512 devices in a mesh: row: 16 (over y_hi, x), pair: 32 (over y_lo, z, core).
Axes of the slice: x: 4, y: 8 (y_hi: 4, y_lo: 2; y = y_hi * 2 + y_lo), z: 8, core: 2. Of those that a mesh axis runs over, the one named last changes fastest.
Arguments:
- embedding: float32 [32768, 8192], P(('row', 'pair')), may hold values from -54 to 54
- pairing: int32 [64], replicated, may hold values from 0 to 63, each once
Outputs:
- rotated: float32 [32768, 8192], P('row', 'pair')
The draws below stay inside these ranges and needn't reach their ends.
Inputs may be any that keep to these rules, and one draw needn't show every extreme that they name: `pairing`: each column block index from 0 to 63 appears exactly once.
All inputs are finite; a program needn't handle non-finite values.
Results may differ from the reference program's by a relative error of at most 0.0003.
Values sent between devices are 32-bit elements; how exact they have to be, the bound alone decides.
A program may use at most 64 MiB of HBM per device.

```python
import math
import jax
import jax.numpy as jnp
import numpy as np
from jax import lax

BLOCK = 128
ROUNDS = 3
SWEEPS = 2
SLOTS = 64
ROWS = 32768
COLS = 8192


def draw_embedding(key, part):
    key_one, key_two, key_three = jax.random.split(jax.random.fold_in(key, 11), 3)
    noise_part = jax.random.truncated_normal(key_one, -6.0, 6.0, (ROWS, COLS), jnp.float32)
    row_scale = jnp.exp(jax.random.uniform(key_two, (ROWS, 1), jnp.float32, math.log(0.3), math.log(3.0)))
    col_scale = jnp.exp(jax.random.uniform(key_three, (1, COLS), jnp.float32, math.log(0.3), math.log(3.0)))
    return noise_part * row_scale * col_scale


def setup_inputs(seed: int = 0) -> dict:
    splits = jax.random.split(jax.random.key(seed), 3)
    embedding = draw_embedding(jax.random.fold_in(splits[2], 71), 0)
    pairing = jax.random.permutation(splits[1], SLOTS).astype(jnp.int32)
    return {"embedding": embedding, "pairing": pairing}


def make_rotation(gram_mat, total_rows):
    width = gram_mat.shape[0]
    identity = jnp.eye(width, dtype=gram_mat.dtype)
    current = gram_mat
    accumulated = identity
    for sweep in range(SWEEPS):
        scaled = current / total_rows
        level = jnp.diagonal(scaled) + 1e-06
        spread = level[None, :] - level[:, None]
        generator = scaled * spread / (spread * spread + 0.25 * level[:, None] * level[None, :])
        metric = identity - jnp.dot(generator, generator, precision=lax.Precision.HIGHEST)
        factor = jnp.linalg.cholesky(metric)
        turned_t = lax.linalg.triangular_solve(factor, identity - generator, left_side=True, lower=True)
        step_rot = turned_t.T
        if sweep == 0:
            accumulated = step_rot
        else:
            accumulated = jnp.dot(accumulated, step_rot, precision=lax.Precision.HIGHEST)
        if sweep + 1 < SWEEPS:
            half = jnp.dot(current, step_rot, precision=lax.Precision.HIGHEST)
            current = jnp.dot(step_rot.T, half, precision=lax.Precision.HIGHEST)
    return accumulated

def turn_pair(pair_cols):
    gram_mat = lax.dot_general(pair_cols, pair_cols, (((0,), (0,)), ((), ())), precision=lax.Precision.HIGHEST, preferred_element_type=pair_cols.dtype)
    rotation = make_rotation(gram_mat, ROWS)
    return jnp.dot(pair_cols, rotation, precision=lax.Precision.HIGHEST)

def move_source(slots):
    counter = np.arange(slots)
    source = np.where(counter % 2 == 0, counter - 2, counter + 2).astype(np.int32)
    source[0] = 0
    source[2] = 1
    source[slots - 1] = slots - 2
    return source

def reference(embedding, pairing):
    work = jnp.take(embedding.reshape(ROWS, SLOTS, BLOCK), pairing, axis=1)
    source = jnp.asarray(move_source(SLOTS))
    for round_num in range(ROUNDS):
        pairs = work.reshape(ROWS, SLOTS // 2, 2 * BLOCK).transpose(1, 0, 2)
        pairs = lax.map(turn_pair, pairs)
        work = jnp.take(pairs.transpose(1, 0, 2).reshape(ROWS, SLOTS, BLOCK), source, axis=1)
    return work.reshape(ROWS, COLS)
```

```python
import functools

import jax
import jax.numpy as jnp
from jax import lax
from jax.experimental import pallas as pl
from jax.experimental.pallas import tpu as pltpu
from jax.sharding import PartitionSpec as P

ROUNDS = 3
SWEEPS = 2
F32 = jnp.float32
BF16 = jnp.bfloat16


def halves(a):
    high = a.astype(BF16)
    return high, (a - high.astype(F32)).astype(BF16)


def product(a, b, dims=((1,), (0,))):
    def one(x, y):
        return lax.dot_general(x, y, (dims, ((), ())), preferred_element_type=F32)

    a_high, a_low = a
    b_high, b_low = b
    return one(a_high, b_high) + (one(a_high, b_low) + one(a_low, b_high))


def rotation_kernel(total_rows, gram_ref, rotation_ref, upper_ref, lower_ref, current, basis, level, strict):
    width = gram_ref.shape[0]
    block = width // 2
    rows = lax.broadcasted_iota(jnp.int32, (width, width), 0)
    cols = lax.broadcasted_iota(jnp.int32, (width, width), 1)
    eye = rows == cols
    above = rows < cols

    def diag_row(a):
        return jnp.sum(jnp.where(eye, a, 0.0), axis=0, keepdims=True)

    def diag_col(a):
        return jnp.sum(jnp.where(eye, a, 0.0), axis=1, keepdims=True)

    current[...] = gram_ref[...]
    for sweep in range(SWEEPS):
        scaled = current[...] * (1.0 / total_rows)
        level_row = diag_row(scaled) + 1e-06
        level_col = diag_col(scaled) + 1e-06
        spread = level_row - level_col
        generator = scaled * spread / (spread * spread + 0.25 * level_col * level_row)
        parts = halves(generator)
        square = product(parts, parts)
        basis[...] = jnp.where(eye, 1.0, 0.0) + generator
        level[...] = 1.0 - diag_col(square)
        strict[...] = jnp.where(above, -square, 0.0)
        size = jnp.sum(square * square * jnp.where(above, 1.0, 0.0))

        @pl.when(size > 0.0625)
        def _():
            exact = jnp.dot(generator, generator, precision=lax.Precision.HIGHEST, preferred_element_type=F32)
            current_metric = jnp.where(eye, 1.0, 0.0) - exact
            strict[...] = 0.5 * (current_metric + current_metric.T)

            def step(k, _):
                pivot_row = strict[pl.ds(k, 1), :]
                lane = lax.broadcasted_iota(jnp.int32, (1, width), 1)
                pivot = jnp.sum(jnp.where(lane == k, pivot_row, 0.0), axis=1, keepdims=True)
                after = jnp.where(lane > k, pivot_row / pivot, 0.0)
                metric = strict[...]
                pivot_col = jnp.sum(jnp.where(cols == k, metric, 0.0), axis=1, keepdims=True)
                strict[...] = metric - pivot_col * after
                turned = basis[...]
                basis_col = jnp.sum(jnp.where(cols == k, turned, 0.0), axis=1, keepdims=True)
                basis[...] = turned - basis_col * after
                return 0

            lax.fori_loop(0, width, step, 0)
            level[...] = diag_col(strict[...])
            strict[...] = jnp.zeros_like(strict)

        def eliminate(state):
            _, count = state
            upper = strict[...]
            scale = level[...]
            ratio = upper / scale
            ratio_parts = halves(ratio)
            turned = basis[...]
            basis[...] = turned - product(halves(turned), ratio_parts)
            size_now = jnp.sum(upper * upper)

            @pl.when(size_now > 1e-06)
            def _():
                second = product(halves(upper), ratio_parts)
                mixed = product(halves(ratio.T), halves(0.5 * upper - second))
                level[...] = scale - 2.0 * diag_col(mixed)
                strict[...] = jnp.where(above, -(second + mixed + mixed.T), 0.0)

            return size_now, count + 1

        lax.while_loop(
            lambda state: jnp.logical_and(state[0] > 1e-06, state[1] < width),
            eliminate,
            (jnp.float32(1.0), jnp.int32(0)),
        )
        level_out = jnp.sum(jnp.where(eye, jnp.broadcast_to(level[...], (width, width)), 0.0), axis=0, keepdims=True)
        step_rot = basis[...] * lax.rsqrt(level_out)
        step_parts = halves(step_rot)
        half = product(halves(current[...]), step_parts)
        if sweep == 0:
            rotation_ref[...] = step_rot
        else:
            rotation_ref[...] = product(halves(rotation_ref[...]), step_parts)
        if sweep + 1 < SWEEPS:
            current[...] = product(halves(step_rot.T), halves(half))
        else:
            turned_t = step_rot.T
            upper_ref[...] = product(halves(turned_t[:block]), halves(half[:, :block]))
            lower_ref[...] = product(halves(turned_t[block:]), halves(half[:, block:]))


def make_rotation(gram, total_rows):
    width = gram.shape[0]
    block = width // 2
    return pl.pallas_call(
        functools.partial(rotation_kernel, total_rows),
        out_shape=(
            jax.ShapeDtypeStruct((width, width), F32),
            jax.ShapeDtypeStruct((block, block), F32),
            jax.ShapeDtypeStruct((block, block), F32),
        ),
        in_specs=[pl.BlockSpec(memory_space=pltpu.VMEM)],
        out_specs=(pl.BlockSpec(memory_space=pltpu.VMEM),) * 3,
        scratch_shapes=[
            pltpu.VMEM((width, width), F32),
            pltpu.VMEM((width, width), F32),
            pltpu.VMEM((width, 1), F32),
            pltpu.VMEM((width, width), F32),
        ],
        name="rotation",
    )(gram)


def gathered_total(array, axis):
    return lax.all_gather(array, axis).sum(0)


def shifted(block, axis, distance):
    devices = range(lax.axis_size(axis))
    route = [(i - distance, i) for i in devices if i - distance in devices]
    return lax.ppermute(block, axis, route)


def sent_to_all(array, axis):
    devices = lax.axis_size(axis)
    return lax.all_to_all(
        jnp.broadcast_to(array[None], (devices, *array.shape)), axis, 0, 0, tiled=True
    )


def taken_together(array, axis):
    return sent_to_all(array, axis).sum(axis=0)


def inner_rows(left_side, right_side):
    return lax.dot_general(
        left_side,
        right_side,
        (((0,), (0,)), ((), ())),
        precision=lax.Precision.HIGHEST,
        preferred_element_type=jnp.float32,
    )


def full_gram(upper_block, lower_block):
    pair_cols = jnp.concatenate([upper_block, lower_block], axis=1)
    return gathered_total(inner_rows(pair_cols, pair_cols), "row")


def move_blocks(upper_load, lower_load, position, last_index):
    sent_on = jnp.where(position == 0, lower_load, upper_load)
    came_on = shifted(sent_on, "pair", 1)
    came_back = shifted(lower_load, "pair", -1)
    new_upper = jnp.where(position == 0, upper_load, came_on)
    new_lower = jnp.where(position == last_index, upper_load, came_back)
    return (new_upper, new_lower)


def body(embedding, pairing):
    sub_rows, columns = embedding.shape
    slots = pairing.shape[0]
    block = columns // slots
    ordered = jnp.take(embedding.reshape(sub_rows, slots, block), pairing, axis=1).reshape(
        sub_rows, columns
    )
    local = lax.all_to_all(ordered, "pair", split_axis=1, concat_axis=0, tiled=True)
    rows_here = local.shape[0]
    total_rows = rows_here * lax.axis_size("row")
    position = lax.axis_index("pair")
    last_index = lax.axis_size("pair") - 1
    upper_block = local[:, :block]
    lower_block = local[:, block:]
    gram_mat = full_gram(upper_block, lower_block)
    for round_num in range(ROUNDS):
        rotation, upper_gram, lower_gram = make_rotation(gram_mat, total_rows)
        pair_cols = jnp.concatenate([upper_block, lower_block], axis=1)
        turned = jnp.dot(
            pair_cols, rotation, precision=lax.Precision.HIGHEST, preferred_element_type=jnp.float32
        )
        upper_block = turned[:, :block]
        lower_block = turned[:, block:]
        if round_num + 1 < ROUNDS:
            upper_load = jnp.concatenate([upper_block, upper_gram], axis=0)
            lower_load = jnp.concatenate([lower_block, lower_gram], axis=0)
            upper_load, lower_load = move_blocks(upper_load, lower_load, position, last_index)
            upper_block = upper_load[:rows_here]
            upper_gram = upper_load[rows_here:]
            lower_block = lower_load[:rows_here]
            lower_gram = lower_load[rows_here:]
            cross = taken_together(inner_rows(upper_block, lower_block), "row")
            gram_mat = jnp.concatenate(
                [
                    jnp.concatenate([upper_gram, cross], axis=1),
                    jnp.concatenate([cross.T, lower_gram], axis=1),
                ],
                axis=0,
            )
        else:
            upper_block, lower_block = move_blocks(upper_block, lower_block, position, last_index)
    return jnp.concatenate([upper_block, lower_block], axis=1)


def solution(mesh):
    in_specs = (P(("row", "pair"), None), P())
    out_specs = P("row", "pair")
    return jax.shard_map(body, mesh=mesh, in_specs=in_specs, out_specs=out_specs, check_vma=False)
```

```python
import functools

import jax
import jax.numpy as jnp
from jax import lax
from jax.experimental import pallas as pl
from jax.experimental.pallas import tpu as pltpu
from jax.sharding import PartitionSpec as P

ROUNDS = 3
SWEEPS = 2
F32 = jnp.float32
BF16 = jnp.bfloat16


def halves(a):
    high = a.astype(BF16)
    return high, (a - high.astype(F32)).astype(BF16)


def product(a, b, dims=((1,), (0,))):
    def one(x, y):
        return lax.dot_general(x, y, (dims, ((), ())), preferred_element_type=F32)

    a_high, a_low = a
    b_high, b_low = b
    return one(a_high, b_high) + (one(a_high, b_low) + one(a_low, b_high))


def rotation_kernel(total_rows, gram_ref, rotation_ref, upper_ref, lower_ref, current, basis, level, strict):
    width = gram_ref.shape[0]
    block = width // 2
    rows = lax.broadcasted_iota(jnp.int32, (width, width), 0)
    cols = lax.broadcasted_iota(jnp.int32, (width, width), 1)
    eye = rows == cols
    above = rows < cols

    def diag_row(a):
        return jnp.sum(jnp.where(eye, a, 0.0), axis=0, keepdims=True)

    def diag_col(a):
        return jnp.sum(jnp.where(eye, a, 0.0), axis=1, keepdims=True)

    current[...] = gram_ref[...]
    for sweep in range(SWEEPS):
        scaled = current[...] * (1.0 / total_rows)
        level_row = diag_row(scaled) + 1e-06
        level_col = diag_col(scaled) + 1e-06
        spread = level_row - level_col
        generator = scaled * spread / (spread * spread + 0.25 * level_col * level_row)
        parts = halves(generator)
        square = product(parts, parts)
        basis[...] = jnp.where(eye, 1.0, 0.0) + generator
        level[...] = 1.0 - diag_col(square)
        strict[...] = jnp.where(above, -square, 0.0)
        size = jnp.sum(square * square * jnp.where(above, 1.0, 0.0))

        @pl.when(size > 0.0625)
        def _():
            exact = jnp.dot(generator, generator, precision=lax.Precision.HIGHEST, preferred_element_type=F32)
            current_metric = jnp.where(eye, 1.0, 0.0) - exact
            strict[...] = 0.5 * (current_metric + current_metric.T)

            def step(k, _):
                pivot_row = strict[pl.ds(k, 1), :]
                lane = lax.broadcasted_iota(jnp.int32, (1, width), 1)
                pivot = jnp.sum(jnp.where(lane == k, pivot_row, 0.0), axis=1, keepdims=True)
                after = jnp.where(lane > k, pivot_row / pivot, 0.0)
                metric = strict[...]
                pivot_col = jnp.sum(jnp.where(cols == k, metric, 0.0), axis=1, keepdims=True)
                strict[...] = metric - pivot_col * after
                turned = basis[...]
                basis_col = jnp.sum(jnp.where(cols == k, turned, 0.0), axis=1, keepdims=True)
                basis[...] = turned - basis_col * after
                return 0

            lax.fori_loop(0, width, step, 0)
            level[...] = diag_col(strict[...])
            strict[...] = jnp.zeros_like(strict)

        def eliminate(state):
            _, count = state
            upper = strict[...]
            scale = level[...]
            ratio = upper / scale
            ratio_parts = halves(ratio)
            turned = basis[...]
            basis[...] = turned - product(halves(turned), ratio_parts)
            size_now = jnp.sum(upper * upper)

            @pl.when(size_now > 1e-06)
            def _():
                second = product(halves(upper), ratio_parts)
                mixed = product(halves(ratio.T), halves(0.5 * upper - second))
                level[...] = scale - 2.0 * diag_col(mixed)
                strict[...] = jnp.where(above, -(second + mixed + mixed.T), 0.0)

            return size_now, count + 1

        lax.while_loop(
            lambda state: jnp.logical_and(state[0] > 1e-06, state[1] < width),
            eliminate,
            (jnp.float32(1.0), jnp.int32(0)),
        )
        level_out = jnp.sum(jnp.where(eye, jnp.broadcast_to(level[...], (width, width)), 0.0), axis=0, keepdims=True)
        step_rot = basis[...] * lax.rsqrt(level_out)
        step_parts = halves(step_rot)
        half = product(halves(current[...]), step_parts)
        if sweep == 0:
            rotation_ref[...] = step_rot
        else:
            rotation_ref[...] = product(halves(rotation_ref[...]), step_parts)
        if sweep + 1 < SWEEPS:
            current[...] = product(halves(step_rot.T), halves(half))
        else:
            turned_t = step_rot.T
            upper_ref[...] = product(halves(turned_t[:block]), halves(half[:, :block]))
            lower_ref[...] = product(halves(turned_t[block:]), halves(half[:, block:]))


def make_rotation(gram, total_rows):
    width = gram.shape[0]
    block = width // 2
    return pl.pallas_call(
        functools.partial(rotation_kernel, total_rows),
        out_shape=(
            jax.ShapeDtypeStruct((width, width), F32),
            jax.ShapeDtypeStruct((block, block), F32),
            jax.ShapeDtypeStruct((block, block), F32),
        ),
        in_specs=[pl.BlockSpec(memory_space=pltpu.VMEM)],
        out_specs=(pl.BlockSpec(memory_space=pltpu.VMEM),) * 3,
        scratch_shapes=[
            pltpu.VMEM((width, width), F32),
            pltpu.VMEM((width, width), F32),
            pltpu.VMEM((width, 1), F32),
            pltpu.VMEM((width, width), F32),
        ],
        compiler_params=pltpu.CompilerParams(vmem_limit_bytes=14 * 2**20),
        name="rotation",
    )(gram)


MESH = pl.DeviceIdType.MESH
CHUNK = 256
GRANT = 14 * 2**20


def greet(peers):
    barrier = pltpu.get_barrier_semaphore()
    for peer, wanted in peers:
        if wanted is None:
            pl.semaphore_signal(barrier, inc=1, device_id=peer, device_id_type=MESH)
        else:

            @pl.when(wanted)
            def _(peer=peer):
                pl.semaphore_signal(barrier, inc=1, device_id=peer, device_id_type=MESH)


def met(count):
    pl.semaphore_wait(pltpu.get_barrier_semaphore(), count)


def row_place(grid):
    deep, wide = grid
    me = lax.axis_index("row")
    return me // wide, me % wide


def row_peers(grid):
    deep, wide = grid
    down, across = row_place(grid)
    peers = [({"row": down * wide + (across + j) % wide}, None) for j in range(1, wide)]
    return peers + [({"row": (down + j) % deep * wide + across}, None) for j in range(1, deep)]


def row_total(grid, part, total, slots, sums, send, recv):
    deep, wide = grid
    down, across = row_place(grid)
    piece = part.shape[0] // wide
    mine = pl.ds(pl.multiple_of(across * piece, 8), piece)

    def across_peer(j):
        return {"row": down * wide + (across + j) % wide}

    scatter = []
    for j in range(1, wide):
        theirs = pl.ds(pl.multiple_of((across + j) % wide * piece, 8), piece)
        scatter.append(
            pltpu.make_async_remote_copy(
                part.at[theirs], slots.at[j - 1], send.at[0, j], recv.at[0, j], across_peer(j), MESH
            )
        )
        scatter[-1].start()
    for copy in scatter:
        copy.wait_recv()
    value = part[mine, :]
    for j in range(1, wide):
        value = value + slots[j - 1]
    sums[down] = value
    exchange = []
    for j in range(1, deep):
        peer = {"row": (down + j) % deep * wide + across}
        exchange.append(
            pltpu.make_async_remote_copy(
                sums.at[down], sums.at[down], send.at[1, j], recv.at[1, j], peer, MESH
            )
        )
        exchange[-1].start()
    for copy in exchange:
        copy.wait_recv()
    value = sums[0]
    for j in range(1, deep):
        value = value + sums[j]
    total[mine, :] = value
    gather = []
    for j in range(1, wide):
        gather.append(
            pltpu.make_async_remote_copy(
                total.at[mine], total.at[mine], send.at[2, j], recv.at[2, j], across_peer(j), MESH
            )
        )
        gather[-1].start()
    for copy in gather:
        copy.wait_recv()
    for copy in scatter + exchange + gather:
        copy.wait_send()


def total_scratch(grid, rows, block):
    deep, wide = grid
    steps = max(grid)
    return [
        pltpu.VMEM((rows, block), F32),
        pltpu.VMEM((rows, block), F32),
        pltpu.VMEM((wide, rows // wide, block), F32),
        pltpu.VMEM((deep, rows // wide, block), F32),
        pltpu.SemaphoreType.DMA((3, steps)),
        pltpu.SemaphoreType.DMA((3, steps)),
    ]


def turn_and_move(
    blocks, rotation, fresh, ahead, back, send, recv, spin_high, spin_low, first, last, position, count
):
    block = blocks.shape[2]
    chunks = blocks.shape[1] // CHUNK
    high, low = halves(rotation[...])
    spin_high[...] = high
    spin_low[...] = low

    def copies(c):
        rows = pl.ds(pl.multiple_of(c * CHUNK, CHUNK), CHUNK)
        onward = pltpu.make_async_remote_copy(
            ahead.at[rows], fresh.at[0, rows], send.at[0, c], recv.at[0, c], {"pair": position + 1}, MESH
        )
        return rows, onward, pltpu.make_async_remote_copy(
            back.at[rows], fresh.at[1, rows], send.at[1, c], recv.at[1, c], {"pair": position - 1}, MESH
        )

    def turn(c, _):
        rows, _, _ = copies(c)
        pair = jnp.concatenate([blocks[0, rows, :], blocks[1, rows, :]], axis=1)
        turned = product(halves(pair), (spin_high[...], spin_low[...]))
        upper, lower = turned[:, :block], turned[:, block:]
        ahead[rows, :] = jnp.where(first, lower, upper)
        back[rows, :] = lower

        @pl.when(first)
        def _():
            fresh[0, rows, :] = upper

        @pl.when(last)
        def _():
            fresh[1, rows, :] = upper

        return 0

    def leave(c, _):
        _, onward, backward = copies(c)

        @pl.when(jnp.logical_not(last))
        def _():
            onward.start()

        @pl.when(jnp.logical_not(first))
        def _():
            backward.start()

        return 0

    def turn_and_leave(c, _):
        turn(c, 0)
        return leave(c, 0)

    early = chunks // 2
    lax.fori_loop(0, early, turn, 0)
    met(count)
    lax.fori_loop(0, early, leave, 0)
    lax.fori_loop(early, chunks, turn_and_leave, 0)

    def arrive(c):
        _, onward, backward = copies(c)

        @pl.when(jnp.logical_not(first))
        def _():
            onward.wait_recv()

        @pl.when(jnp.logical_not(last))
        def _():
            backward.wait_recv()

    def finish():
        def left(c, _):
            _, onward, backward = copies(c)

            @pl.when(jnp.logical_not(last))
            def _():
                onward.wait_send()

            @pl.when(jnp.logical_not(first))
            def _():
                backward.wait_send()

            return 0

        lax.fori_loop(0, chunks, left, 0)

    return arrive, finish


def pair_place():
    position = lax.axis_index("pair")
    first = position == 0
    last = position == lax.axis_size("pair") - 1
    count = jnp.where(first, 0, 1) + jnp.where(last, 0, 1)
    peers = [
        ({"pair": position + 1}, jnp.logical_not(last)),
        ({"pair": position - 1}, jnp.logical_not(first)),
    ]
    return position, first, last, peers, count


def round_kernel(
    grid, blocks, rotation, upper_gram, lower_gram, fresh, gram,
    ahead, back, ahead_gram, back_gram, spin_high, spin_low, send, recv, gram_send, gram_recv,
    part, total, slots, sums, sum_send, sum_recv,
):
    position, first, last, peers, count = pair_place()
    block = blocks.shape[2]
    across = row_peers(grid)
    greet(peers + across)
    ahead_gram[...] = jnp.where(first, lower_gram[...], upper_gram[...])
    back_gram[...] = lower_gram[...]

    @pl.when(first)
    def _():
        gram[:block, :block] = upper_gram[...]

    @pl.when(last)
    def _():
        gram[block:, block:] = upper_gram[...]

    arrive, finish = turn_and_move(
        blocks, rotation, fresh, ahead, back, send, recv, spin_high, spin_low, first, last, position,
        count + len(across),
    )
    onward = pltpu.make_async_remote_copy(
        ahead_gram, gram.at[pl.ds(0, block), pl.ds(0, block)], gram_send.at[0], gram_recv.at[0],
        {"pair": position + 1}, MESH,
    )
    backward = pltpu.make_async_remote_copy(
        back_gram, gram.at[pl.ds(block, block), pl.ds(block, block)], gram_send.at[1], gram_recv.at[1],
        {"pair": position - 1}, MESH,
    )

    @pl.when(jnp.logical_not(last))
    def _():
        onward.start()

    @pl.when(jnp.logical_not(first))
    def _():
        backward.start()

    part[...] = jnp.zeros_like(part)

    def cross(c, _):
        arrive(c)
        rows = pl.ds(pl.multiple_of(c * CHUNK, CHUNK), CHUNK)
        part[...] += product(halves(fresh[0, rows, :]), halves(fresh[1, rows, :]), ((0,), (0,)))
        return 0

    lax.fori_loop(0, blocks.shape[1] // CHUNK, cross, 0)
    row_total(grid, part, total, slots, sums, sum_send, sum_recv)
    gram[:block, block:] = total[...]
    gram[block:, :block] = total[...].T

    @pl.when(jnp.logical_not(first))
    def _():
        onward.wait_recv()
        backward.wait_send()

    @pl.when(jnp.logical_not(last))
    def _():
        backward.wait_recv()
        onward.wait_send()

    finish()


def last_kernel(blocks, rotation, fresh, ahead, back, spin_high, spin_low, send, recv):
    position, first, last, peers, count = pair_place()
    greet(peers)
    arrive, finish = turn_and_move(
        blocks, rotation, fresh, ahead, back, send, recv, spin_high, spin_low, first, last, position, count
    )

    def take(c, _):
        arrive(c)
        return 0

    lax.fori_loop(0, blocks.shape[1] // CHUNK, take, 0)
    finish()


def move_scratch(rows, block):
    width = 2 * block
    chunks = rows // CHUNK
    return (
        [pltpu.VMEM((rows, block), F32), pltpu.VMEM((rows, block), F32)],
        [pltpu.VMEM((width, width), BF16), pltpu.VMEM((width, width), BF16)],
        [pltpu.SemaphoreType.DMA((2, chunks)), pltpu.SemaphoreType.DMA((2, chunks))],
    )


VMEM = pl.BlockSpec(memory_space=pltpu.VMEM)


def next_round(blocks, rotation, upper_gram, lower_gram, grid):
    _, rows, block = blocks.shape
    loads, spins, sems = move_scratch(rows, block)
    return pl.pallas_call(
        functools.partial(round_kernel, grid),
        out_shape=(
            jax.ShapeDtypeStruct(blocks.shape, F32),
            jax.ShapeDtypeStruct((2 * block, 2 * block), F32),
        ),
        in_specs=[VMEM] * 4,
        out_specs=(VMEM, VMEM),
        scratch_shapes=loads
        + [pltpu.VMEM((block, block), F32), pltpu.VMEM((block, block), F32)]
        + spins
        + sems
        + [pltpu.SemaphoreType.DMA((2,)), pltpu.SemaphoreType.DMA((2,))]
        + total_scratch(grid, block, block),
        compiler_params=pltpu.CompilerParams(collective_id=1, has_side_effects=True, vmem_limit_bytes=GRANT),
        name="next_round",
    )(blocks, rotation, upper_gram, lower_gram)


def last_round(blocks, rotation):
    _, rows, block = blocks.shape
    loads, spins, sems = move_scratch(rows, block)
    return pl.pallas_call(
        last_kernel,
        out_shape=jax.ShapeDtypeStruct(blocks.shape, F32),
        in_specs=[VMEM] * 2,
        out_specs=VMEM,
        scratch_shapes=loads + spins + sems,
        compiler_params=pltpu.CompilerParams(collective_id=2, has_side_effects=True, vmem_limit_bytes=GRANT),
        name="last_round",
    )(blocks, rotation)


def pick_kernel(embedding, pairing, picked, sems):
    slots = pairing.shape[0]
    block = picked.shape[3]

    def copy(slot):
        source = pl.ds(pl.multiple_of(pairing[slot] * block, block), block)
        return pltpu.make_async_copy(embedding.at[:, source], picked.at[slot // 2, slot % 2], sems.at[slot])

    def start(slot, _):
        copy(slot).start()
        return 0

    def wait(slot, _):
        copy(slot).wait()
        return 0

    lax.fori_loop(0, slots, start, 0)
    lax.fori_loop(0, slots, wait, 0)


def pick(embedding, pairing):
    sub_rows, columns = embedding.shape
    slots = pairing.shape[0]
    return pl.pallas_call(
        pick_kernel,
        out_shape=jax.ShapeDtypeStruct((slots // 2, 2, sub_rows, columns // slots), F32),
        in_specs=[pl.BlockSpec(memory_space=pl.ANY), pl.BlockSpec(memory_space=pltpu.SMEM)],
        out_specs=VMEM,
        scratch_shapes=[pltpu.SemaphoreType.DMA((slots,))],
        compiler_params=pltpu.CompilerParams(vmem_limit_bytes=GRANT),
        name="pick",
    )(embedding, pairing)


def deal_kernel(
    grid, cut, outgoing, blocks, gram, relayed, send, recv, relay_send, relay_recv, own,
    part, total, slots, sums, sum_send, sum_recv,
):
    tall, ring, cores = cut
    sub_rows = outgoing.shape[2]
    block = blocks.shape[2]
    devices = lax.axis_size("pair")
    me = lax.axis_index("pair")
    core, turn, side = me % cores, me // cores % ring, me // (cores * ring)
    halfway = ring // 2
    group = tall * cores

    def device(there_side, there_turn, there_core):
        return (there_side % tall * ring + (there_turn + 2 * ring) % ring) * cores + there_core % cores

    def target_of(far, near):
        return device(side + near // cores, turn + far, core + near % cores)

    def rows_of(index):
        return pl.ds(pl.multiple_of(index * sub_rows, sub_rows), sub_rows)

    def far_of(order):
        away = (order + 1) // 2
        return halfway + away - 2 * away * (order % 2)

    def copy_at(far, near):
        target = target_of(far, near)
        step = far * group + near
        return pltpu.make_async_remote_copy(
            outgoing.at[target], blocks.at[:, rows_of(me), :], send.at[step], recv.at[step], {"pair": target}, MESH
        )

    def relay_at(over):
        near = over * cores + 1
        target = target_of(halfway, near)
        between = device(side + over, turn - halfway // 2, core + 1)
        step = halfway * group + near
        return pltpu.make_async_remote_copy(
            outgoing.at[target], relayed.at[over], send.at[step], relay_recv.at[over], {"pair": between}, MESH
        )

    def forward_at(over):
        step = halfway * group + over * cores + 1
        origin = device(side - over + tall, turn + halfway // 2, core + 1)
        return pltpu.make_async_remote_copy(
            relayed.at[over], blocks.at[:, rows_of(origin), :], relay_send.at[over], recv.at[step],
            {"pair": device(side, turn - halfway // 2, core)}, MESH,
        )

    barrier = pltpu.get_barrier_semaphore()

    def call(step, _):
        target = target_of(step // group, step % group)
        pl.semaphore_signal(barrier, inc=1, device_id={"pair": target}, device_id_type=MESH)
        return 0

    lax.fori_loop(1, devices, call, 0)
    across = row_peers(grid)
    greet(across)
    keep = pltpu.make_async_copy(outgoing.at[me], blocks.at[:, rows_of(me), :], own)
    keep.start()
    met(devices - 1 + len(across))
    for over in range(tall):
        relay_at(over).start()
        for there in range(0, cores, 2):
            copy_at(halfway, over * cores + there).start()

    def send_all(order, _):
        for near in range(group):
            copy_at(far_of(order), near).start()
        return 0

    lax.fori_loop(1, ring - 1, send_all, 0)
    for near in range(1, group):
        copy_at(0, near).start()
    for over in range(tall):
        relay_at(over).wait_recv()
        forward_at(over).start()
    keep.wait()
    part[...] = jnp.zeros_like(part)

    def add(order, _):
        far = far_of(order)
        for near in range(group):

            @pl.when(far * group + near > 0)
            def _(near=near):
                copy_at(far, near).wait_recv()

        for there in range(tall):
            source = (there * ring + (turn - far + ring) % ring) * cores
            rows = pl.ds(pl.multiple_of(source * sub_rows, sub_rows * cores), sub_rows * cores)
            high, low = halves(jnp.concatenate([blocks[0, rows, :], blocks[1, rows, :]], axis=1))

            def one(x, y):
                return lax.dot_general(x, y, (((0,), (0,)), ((), ())), preferred_element_type=F32)

            main, side_part = one(high, high), one(high, low)
            whole = main + (side_part + side_part.T)
            part[:block, :] += whole[:block, :block]
            part[block : 2 * block, :] += whole[:block, block:]
            part[2 * block :, :] += whole[block:, block:]
        return 0

    lax.fori_loop(0, ring, add, 0)
    row_total(grid, part, total, slots, sums, sum_send, sum_recv)
    gram[:block, :block] = total[:block, :]
    gram[:block, block:] = total[block : 2 * block, :]
    gram[block:, :block] = total[block : 2 * block, :].T
    gram[block:, block:] = total[2 * block :, :]

    def sent(step, _):
        copy_at(step // group, step % group).wait_send()
        return 0

    lax.fori_loop(1, devices, sent, 0)
    for over in range(tall):
        forward_at(over).wait_send()


def deal(picked, grid, cut):
    devices, _, sub_rows, block = picked.shape
    return pl.pallas_call(
        functools.partial(deal_kernel, grid, cut),
        out_shape=(
            jax.ShapeDtypeStruct((2, sub_rows * devices, block), F32),
            jax.ShapeDtypeStruct((2 * block, 2 * block), F32),
        ),
        in_specs=[VMEM],
        out_specs=(VMEM, VMEM),
        scratch_shapes=[
            pltpu.VMEM((cut[0], 2, sub_rows, block), F32),
            pltpu.SemaphoreType.DMA((devices,)),
            pltpu.SemaphoreType.DMA((devices,)),
            pltpu.SemaphoreType.DMA((cut[0],)),
            pltpu.SemaphoreType.DMA((cut[0],)),
            pltpu.SemaphoreType.DMA,
        ]
        + total_scratch(grid, 3 * block, block),
        compiler_params=pltpu.CompilerParams(collective_id=0, has_side_effects=True, vmem_limit_bytes=GRANT),
        name="deal",
    )(picked)


def join_kernel(blocks, joined):
    block = blocks.shape[2]
    joined[:, :block] = blocks[0]
    joined[:, block:] = blocks[1]


def join(blocks):
    _, rows, block = blocks.shape
    return pl.pallas_call(
        join_kernel,
        grid=(rows // CHUNK,),
        out_shape=jax.ShapeDtypeStruct((rows, 2 * block), F32),
        in_specs=[pl.BlockSpec((2, CHUNK, block), lambda i: (0, i, 0))],
        out_specs=pl.BlockSpec((CHUNK, 2 * block), lambda i: (i, 0)),
        compiler_params=pltpu.CompilerParams(vmem_limit_bytes=GRANT),
        name="join",
    )(blocks)


def cuts():
    grids = {16: (4, 4), 4: (2, 2)}
    pairs = {32: (2, 8, 2), 4: (1, 2, 2)}
    return grids[lax.axis_size("row")], pairs[lax.axis_size("pair")]


def body(embedding, pairing):
    grid, cut = cuts()
    blocks, gram = deal(pick(embedding, pairing), grid, cut)
    total_rows = blocks.shape[1] * lax.axis_size("row")
    for round_num in range(ROUNDS):
        rotation, upper_gram, lower_gram = make_rotation(gram, total_rows)
        if round_num + 1 < ROUNDS:
            blocks, gram = next_round(blocks, rotation, upper_gram, lower_gram, grid)
        else:
            blocks = last_round(blocks, rotation)
    return join(blocks)


def solution(mesh):
    in_specs = (P(("row", "pair"), None), P())
    out_specs = P("row", "pair")
    return jax.shard_map(body, mesh=mesh, in_specs=in_specs, out_specs=out_specs, check_vma=False)
```

```python
import functools

import jax
import jax.numpy as jnp
from jax import lax
from jax.experimental import pallas as pl
from jax.experimental.pallas import tpu as pltpu
from jax.sharding import PartitionSpec as P

ROUNDS = 3
SWEEPS = 2
F32 = jnp.float32
BF16 = jnp.bfloat16


def halves(a):
    high = a.astype(BF16)
    return high, (a - high.astype(F32)).astype(BF16)


def product(a, b, dims=((1,), (0,))):
    def one(x, y):
        return lax.dot_general(x, y, (dims, ((), ())), preferred_element_type=F32)

    a_high, a_low = a
    b_high, b_low = b
    return one(a_high, b_high) + (one(a_high, b_low) + one(a_low, b_high))


def rotation_kernel(total_rows, gram_ref, rotation_ref, upper_ref, lower_ref, current, basis, level, strict):
    width = gram_ref.shape[0]
    block = width // 2
    rows = lax.broadcasted_iota(jnp.int32, (width, width), 0)
    cols = lax.broadcasted_iota(jnp.int32, (width, width), 1)
    eye = rows == cols
    above = rows < cols

    def diag_row(a):
        return jnp.sum(jnp.where(eye, a, 0.0), axis=0, keepdims=True)

    def diag_col(a):
        return jnp.sum(jnp.where(eye, a, 0.0), axis=1, keepdims=True)

    current[...] = gram_ref[...]
    for sweep in range(SWEEPS):
        scaled = current[...] * (1.0 / total_rows)
        level_row = diag_row(scaled) + 1e-06
        level_col = diag_col(scaled) + 1e-06
        spread = level_row - level_col
        generator = scaled * spread / (spread * spread + 0.25 * level_col * level_row)
        parts = halves(generator)
        square = product(parts, parts)
        basis[...] = jnp.where(eye, 1.0, 0.0) + generator
        level[...] = 1.0 - diag_col(square)
        strict[...] = jnp.where(above, -square, 0.0)
        size = jnp.sum(square * square * jnp.where(above, 1.0, 0.0))

        @pl.when(size > 0.0625)
        def _():
            exact = jnp.dot(generator, generator, precision=lax.Precision.HIGHEST, preferred_element_type=F32)
            current_metric = jnp.where(eye, 1.0, 0.0) - exact
            strict[...] = 0.5 * (current_metric + current_metric.T)

            def step(k, _):
                pivot_row = strict[pl.ds(k, 1), :]
                lane = lax.broadcasted_iota(jnp.int32, (1, width), 1)
                pivot = jnp.sum(jnp.where(lane == k, pivot_row, 0.0), axis=1, keepdims=True)
                after = jnp.where(lane > k, pivot_row / pivot, 0.0)
                metric = strict[...]
                pivot_col = jnp.sum(jnp.where(cols == k, metric, 0.0), axis=1, keepdims=True)
                strict[...] = metric - pivot_col * after
                turned = basis[...]
                basis_col = jnp.sum(jnp.where(cols == k, turned, 0.0), axis=1, keepdims=True)
                basis[...] = turned - basis_col * after
                return 0

            lax.fori_loop(0, width, step, 0)
            level[...] = diag_col(strict[...])
            strict[...] = jnp.zeros_like(strict)

        def eliminate(state):
            _, count = state
            upper = strict[...]
            scale = level[...]
            ratio = upper / scale
            ratio_parts = halves(ratio)
            turned = basis[...]
            basis[...] = turned - product(halves(turned), ratio_parts)
            size_now = jnp.sum(upper * upper)

            @pl.when(size_now > 1e-06)
            def _():
                second = product(halves(upper), ratio_parts)
                mixed = product(halves(ratio.T), halves(0.5 * upper - second))
                level[...] = scale - 2.0 * diag_col(mixed)
                strict[...] = jnp.where(above, -(second + mixed + mixed.T), 0.0)

            return size_now, count + 1

        lax.while_loop(
            lambda state: jnp.logical_and(state[0] > 1e-06, state[1] < width),
            eliminate,
            (jnp.float32(1.0), jnp.int32(0)),
        )
        level_out = jnp.sum(jnp.where(eye, jnp.broadcast_to(level[...], (width, width)), 0.0), axis=0, keepdims=True)
        step_rot = basis[...] * lax.rsqrt(level_out)
        step_parts = halves(step_rot)
        half = product(halves(current[...]), step_parts)
        if sweep == 0:
            rotation_ref[...] = step_rot
        else:
            rotation_ref[...] = product(halves(rotation_ref[...]), step_parts)
        if sweep + 1 < SWEEPS:
            current[...] = product(halves(step_rot.T), halves(half))
        else:
            turned_t = step_rot.T
            upper_ref[...] = product(halves(turned_t[:block]), halves(half[:, :block]))
            lower_ref[...] = product(halves(turned_t[block:]), halves(half[:, block:]))


def make_rotation(gram, total_rows):
    width = gram.shape[0]
    block = width // 2
    return pl.pallas_call(
        functools.partial(rotation_kernel, total_rows),
        out_shape=(
            jax.ShapeDtypeStruct((width, width), F32),
            jax.ShapeDtypeStruct((block, block), F32),
            jax.ShapeDtypeStruct((block, block), F32),
        ),
        in_specs=[pl.BlockSpec(memory_space=pltpu.VMEM)],
        out_specs=(pl.BlockSpec(memory_space=pltpu.VMEM),) * 3,
        scratch_shapes=[
            pltpu.VMEM((width, width), F32),
            pltpu.VMEM((width, width), F32),
            pltpu.VMEM((width, 1), F32),
            pltpu.VMEM((width, width), F32),
        ],
        compiler_params=pltpu.CompilerParams(vmem_limit_bytes=14 * 2**20),
        name="rotation",
    )(gram)


MESH = pl.DeviceIdType.MESH
CHUNK = 256
GRAM_STREAMS = 3
CROSS_STREAMS = 2
DEAL_AHEAD = 5
ROUND_AHEAD = 3
GRANT = 20 * 2**20


def greet(peers):
    barrier = pltpu.get_barrier_semaphore()
    for peer, wanted in peers:
        if wanted is None:
            pl.semaphore_signal(barrier, inc=1, device_id=peer, device_id_type=MESH)
        else:

            @pl.when(wanted)
            def _(peer=peer):
                pl.semaphore_signal(barrier, inc=1, device_id=peer, device_id_type=MESH)


def met(count):
    pl.semaphore_wait(pltpu.get_barrier_semaphore(), count)


def row_place(grid):
    deep, wide = grid
    me = lax.axis_index("row")
    return me // wide, me % wide


def row_peers(grid):
    deep, wide = grid
    down, across = row_place(grid)
    peers = [({"row": down * wide + (across + j) % wide}, None) for j in range(1, wide)]
    return peers + [({"row": (down + j) % deep * wide + across}, None) for j in range(1, deep)]


def row_total(grid, streams, part, total, slots, sums, send, recv):
    deep, wide = grid
    down, across = row_place(grid)
    piece = part.shape[0] // (wide * streams)

    def rows_of(stream, owner):
        return pl.ds(pl.multiple_of((stream * wide + owner) * piece, 8), piece)

    def across_peer(j):
        return {"row": down * wide + (across + j) % wide}

    def scatter(stream, j):
        theirs = rows_of(stream, (across + j) % wide)
        return pltpu.make_async_remote_copy(
            part.at[theirs], slots.at[stream, j], send.at[0, stream, j], recv.at[0, stream, j], across_peer(j), MESH
        )

    def exchange(stream, j):
        mine = sums.at[stream, down]
        peer = {"row": (down + j) % deep * wide + across}
        return pltpu.make_async_remote_copy(
            mine, mine, send.at[1, stream, j], recv.at[1, stream, j], peer, MESH
        )

    def gather(stream, j):
        mine = total.at[rows_of(stream, across)]
        return pltpu.make_async_remote_copy(
            mine, mine, send.at[2, stream, j], recv.at[2, stream, j], across_peer(j), MESH
        )

    for stream in range(streams):
        for j in range(1, wide):
            scatter(stream, j).start()
    for stream in range(streams):
        for j in range(1, wide):
            scatter(stream, j).wait_recv()
        value = part[rows_of(stream, across), :]
        for j in range(1, wide):
            value = value + slots[stream, j]
        sums[stream, down] = value
        for j in range(1, deep):
            exchange(stream, j).start()
    for stream in range(streams):
        for j in range(1, deep):
            exchange(stream, j).wait_recv()
        value = sums[stream, 0]
        for j in range(1, deep):
            value = value + sums[stream, j]
        total[rows_of(stream, across), :] = value
        for j in range(1, wide):
            gather(stream, j).start()
    for stream in range(streams):
        for j in range(1, wide):
            gather(stream, j).wait_recv()
    for stream in range(streams):
        for j in range(1, wide):
            scatter(stream, j).wait_send()
            gather(stream, j).wait_send()
        for j in range(1, deep):
            exchange(stream, j).wait_send()


def total_scratch(grid, streams, rows, block):
    deep, wide = grid
    steps = max(grid)
    piece = rows // (wide * streams)
    return [
        pltpu.VMEM((rows, block), F32),
        pltpu.VMEM((rows, block), F32),
        pltpu.VMEM((streams, wide, piece, block), F32),
        pltpu.VMEM((streams, deep, piece, block), F32),
        pltpu.SemaphoreType.DMA((3, streams, steps)),
        pltpu.SemaphoreType.DMA((3, streams, steps)),
    ]


def chunk_rows(c):
    return pl.ds(pl.multiple_of(c * CHUNK, CHUNK), CHUNK)


def both_ways(onward, backward, first, last, act):
    @pl.when(jnp.logical_not(last))
    def _():
        act(onward)

    @pl.when(jnp.logical_not(first))
    def _():
        act(backward)


def both_arrive(onward, backward, first, last):
    @pl.when(jnp.logical_not(first))
    def _():
        onward.wait_recv()

    @pl.when(jnp.logical_not(last))
    def _():
        backward.wait_recv()


def neighbour_copies(sources, targets, sends, recvs, position):
    def one(way, distance):
        return pltpu.make_async_remote_copy(
            sources[way], targets[way], sends[way], recvs[way], {"pair": position + distance}, MESH
        )

    return one(0, 1), one(1, -1)


def raw_copies(blocks, before, after, send, recv, position):
    source = blocks.at[:, pl.ds(0, before.shape[1])]
    return neighbour_copies((source, source), (before, after), (send.at[0], send.at[1]), (recv.at[0], recv.at[1]), position)


def turn_and_move(
    blocks, before, after, rotation, fresh, ahead, back, own_high, own_low, lent, got, got_high, got_low,
    send, recv, spin_send, spin_recv, first, last, position, count, use,
):
    block = blocks.shape[2]
    chunks = blocks.shape[1] // CHUNK
    there = before.shape[1] // CHUNK
    high, low = halves(rotation[...])
    own_high[...] = high
    own_low[...] = low
    lent[0] = jnp.where(first, rotation[:, block:], rotation[:, :block])
    lent[1] = rotation[:, block:]

    def pair_rows(source, c):
        rows = chunk_rows(c)
        return halves(jnp.concatenate([source[0, rows, :], source[1, rows, :]], axis=1))

    def copies(c):
        rows = chunk_rows(c)
        return neighbour_copies(
            (ahead.at[rows], back.at[rows]),
            (fresh.at[0, rows], fresh.at[1, rows]),
            (send.at[0, c], send.at[1, c]),
            (recv.at[0, c], recv.at[1, c]),
            position,
        )

    def spins():
        return neighbour_copies(
            (lent.at[0], lent.at[1]),
            (got.at[0], got.at[1]),
            (spin_send.at[0], spin_send.at[1]),
            (spin_recv.at[0], spin_recv.at[1]),
            position,
        )

    def turn(c, _):
        rows = chunk_rows(c)
        turned = product(pair_rows(blocks, c), (own_high[...], own_low[...]))
        upper, lower = turned[:, :block], turned[:, block:]
        ahead[rows, :] = jnp.where(first, lower, upper)
        back[rows, :] = lower

        @pl.when(first)
        def _():
            fresh[0, rows, :] = upper

        @pl.when(last)
        def _():
            fresh[1, rows, :] = upper

        return 0

    def leave(c, _):
        both_ways(*copies(c), first, last, lambda copy: copy.start())
        return 0

    def turn_and_leave(c, _):
        turn(c, 0)
        return leave(c, 0)

    early = (chunks + there) // 2
    lax.fori_loop(there, early, turn, 0)
    met(count)
    both_ways(*spins(), first, last, lambda copy: copy.start())
    lax.fori_loop(there, early, leave, 0)
    lax.fori_loop(early, chunks, turn_and_leave, 0)
    both_arrive(*spins(), first, last)

    for way, edge in ((0, first), (1, last)):

        @pl.when(edge)
        def _(way=way):
            got_high[way] = own_high[:, :block]
            got_low[way] = own_low[:, :block]

        @pl.when(jnp.logical_not(edge))
        def _(way=way):
            high, low = halves(got[way])
            got_high[way] = high
            got_low[way] = low

    def turn_there(c, _):
        rows = chunk_rows(c)
        for way, edge, raw in ((0, first, before), (1, last, after)):

            @pl.when(edge)
            def _(way=way):
                fresh[way, rows, :] = product(pair_rows(blocks, c), (got_high[way], got_low[way]))

            @pl.when(jnp.logical_not(edge))
            def _(way=way, raw=raw):
                fresh[way, rows, :] = product(pair_rows(raw, c), (got_high[way], got_low[way]))

        use(c)
        return 0

    lax.fori_loop(0, there, turn_there, 0)

    def take():
        def one(c, _):
            both_arrive(*copies(c), first, last)
            use(c)
            return 0

        lax.fori_loop(there, chunks, one, 0)

    def finish():
        both_ways(*spins(), first, last, lambda copy: copy.wait_send())

        def left(c, _):
            both_ways(*copies(c), first, last, lambda copy: copy.wait_send())
            return 0

        lax.fori_loop(there, chunks, left, 0)

    return take, finish


def pair_place():
    position = lax.axis_index("pair")
    first = position == 0
    last = position == lax.axis_size("pair") - 1
    count = jnp.where(first, 0, 1) + jnp.where(last, 0, 1)
    peers = [
        ({"pair": position + 1}, jnp.logical_not(last)),
        ({"pair": position - 1}, jnp.logical_not(first)),
    ]
    return position, first, last, peers, count


def round_kernel(
    grid, blocks, before, after, rotation, upper_gram, lower_gram, fresh, gram, next_before, next_after,
    ahead, back, own_high, own_low, lent, got, got_high, got_low, send, recv, spin_send, spin_recv,
    ahead_gram, back_gram, gram_send, gram_recv, raw_send, raw_recv,
    part, total, slots, sums, sum_send, sum_recv,
):
    position, first, last, peers, count = pair_place()
    block = blocks.shape[2]
    across = row_peers(grid)
    greet(peers + across)
    ahead_gram[...] = jnp.where(first, lower_gram[...], upper_gram[...])
    back_gram[...] = lower_gram[...]

    @pl.when(first)
    def _():
        gram[:block, :block] = upper_gram[...]

    @pl.when(last)
    def _():
        gram[block:, block:] = upper_gram[...]

    part[...] = jnp.zeros_like(part)

    def cross(c):
        rows = chunk_rows(c)
        part[...] += product(halves(fresh[0, rows, :]), halves(fresh[1, rows, :]), ((0,), (0,)))

    take, finish = turn_and_move(
        blocks, before, after, rotation, fresh, ahead, back, own_high, own_low, lent, got, got_high, got_low,
        send, recv, spin_send, spin_recv, first, last, position, count + len(across), cross,
    )

    def grams():
        return neighbour_copies(
            (ahead_gram, back_gram),
            (gram.at[pl.ds(0, block), pl.ds(0, block)], gram.at[pl.ds(block, block), pl.ds(block, block)]),
            (gram_send.at[0], gram_send.at[1]),
            (gram_recv.at[0], gram_recv.at[1]),
            position,
        )

    def raws():
        return raw_copies(fresh, next_before, next_after, raw_send, raw_recv, position)

    both_ways(*grams(), first, last, lambda copy: copy.start())
    both_ways(*raws(), first, last, lambda copy: copy.start())
    take()
    row_total(grid, CROSS_STREAMS, part, total, slots, sums, sum_send, sum_recv)
    gram[:block, block:] = total[...]
    gram[block:, :block] = total[...].T
    both_arrive(*grams(), first, last)
    both_arrive(*raws(), first, last)
    both_ways(*grams(), first, last, lambda copy: copy.wait_send())
    both_ways(*raws(), first, last, lambda copy: copy.wait_send())
    finish()


def last_kernel(
    blocks, before, after, rotation, fresh,
    ahead, back, own_high, own_low, lent, got, got_high, got_low, send, recv, spin_send, spin_recv,
):
    position, first, last, peers, count = pair_place()
    greet(peers)
    take, finish = turn_and_move(
        blocks, before, after, rotation, fresh, ahead, back, own_high, own_low, lent, got, got_high, got_low,
        send, recv, spin_send, spin_recv, first, last, position, count, lambda c: None,
    )
    take()
    finish()


def move_scratch(rows, block):
    width = 2 * block
    chunks = rows // CHUNK
    return [
        pltpu.VMEM((rows, block), F32),
        pltpu.VMEM((rows, block), F32),
        pltpu.VMEM((width, width), BF16),
        pltpu.VMEM((width, width), BF16),
        pltpu.VMEM((2, width, block), F32),
        pltpu.VMEM((2, width, block), F32),
        pltpu.VMEM((2, width, block), BF16),
        pltpu.VMEM((2, width, block), BF16),
        pltpu.SemaphoreType.DMA((2, chunks)),
        pltpu.SemaphoreType.DMA((2, chunks)),
        pltpu.SemaphoreType.DMA((2,)),
        pltpu.SemaphoreType.DMA((2,)),
    ]


VMEM = pl.BlockSpec(memory_space=pltpu.VMEM)


def raw_shape(chunks, block):
    return jax.ShapeDtypeStruct((2, chunks * CHUNK, block), F32)


def next_round(blocks, before, after, rotation, upper_gram, lower_gram, grid, collective):
    _, rows, block = blocks.shape
    return pl.pallas_call(
        functools.partial(round_kernel, grid),
        out_shape=(
            jax.ShapeDtypeStruct(blocks.shape, F32),
            jax.ShapeDtypeStruct((2 * block, 2 * block), F32),
            raw_shape(ROUND_AHEAD, block),
            raw_shape(ROUND_AHEAD, block),
        ),
        in_specs=[VMEM] * 6,
        out_specs=(VMEM,) * 4,
        scratch_shapes=move_scratch(rows, block)
        + [pltpu.VMEM((block, block), F32), pltpu.VMEM((block, block), F32)]
        + [pltpu.SemaphoreType.DMA((2,))] * 4
        + total_scratch(grid, CROSS_STREAMS, block, block),
        compiler_params=pltpu.CompilerParams(
            collective_id=collective, has_side_effects=True, vmem_limit_bytes=GRANT
        ),
        name="next_round",
    )(blocks, before, after, rotation, upper_gram, lower_gram)


def last_round(blocks, before, after, rotation):
    _, rows, block = blocks.shape
    return pl.pallas_call(
        last_kernel,
        out_shape=jax.ShapeDtypeStruct(blocks.shape, F32),
        in_specs=[VMEM] * 4,
        out_specs=VMEM,
        scratch_shapes=move_scratch(rows, block),
        compiler_params=pltpu.CompilerParams(collective_id=1, has_side_effects=True, vmem_limit_bytes=GRANT),
        name="last_round",
    )(blocks, before, after, rotation)


def pick_kernel(embedding, pairing, picked):
    block = picked.shape[3]

    def one(target, _):
        for half in range(2):
            source = pl.multiple_of(pairing[2 * target + half] * block, block)
            picked[target, half] = embedding[:, pl.ds(source, block)]
        return 0

    lax.fori_loop(0, picked.shape[0], one, 0, unroll=4)


def pick(embedding, pairing):
    sub_rows, columns = embedding.shape
    slots = pairing.shape[0]
    return pl.pallas_call(
        pick_kernel,
        out_shape=jax.ShapeDtypeStruct((slots // 2, 2, sub_rows, columns // slots), F32),
        in_specs=[VMEM, pl.BlockSpec(memory_space=pltpu.SMEM)],
        out_specs=VMEM,
        compiler_params=pltpu.CompilerParams(vmem_limit_bytes=GRANT),
        name="pick",
    )(embedding, pairing)


def deal_kernel(
    grid, cut, outgoing, blocks, gram, before, after, send, recv, own, raw_send, raw_recv,
    part, total, slots, sums, sum_send, sum_recv,
):
    tall, ring, cores = cut
    sub_rows = outgoing.shape[2]
    block = blocks.shape[2]
    devices = lax.axis_size("pair")
    me = lax.axis_index("pair")
    core, turn, side = me % cores, me // cores % ring, me // (cores * ring)
    halfway = ring // 2
    group = tall * cores

    def device(there_side, there_turn, there_core):
        return (there_side % tall * ring + (there_turn + 2 * ring) % ring) * cores + there_core % cores

    def target_of(far, near):
        return device(side + near // cores, turn + far, core + near % cores)

    def rows_of(index):
        return pl.ds(pl.multiple_of(index * sub_rows, sub_rows), sub_rows)

    def far_of(order):
        away = (order + 1) // 2
        return halfway + away - 2 * away * (order % 2)

    def copy_at(far, near):
        target = target_of(far, near)
        step = far * group + near
        return pltpu.make_async_remote_copy(
            outgoing.at[target], blocks.at[:, rows_of(me), :], send.at[step], recv.at[step], {"pair": target}, MESH
        )

    barrier = pltpu.get_barrier_semaphore()

    def call(step, _):
        target = target_of(step // group, step % group)
        pl.semaphore_signal(barrier, inc=1, device_id={"pair": target}, device_id_type=MESH)
        return 0

    lax.fori_loop(1, devices, call, 0)
    across = row_peers(grid)
    greet(across)
    keep = pltpu.make_async_copy(outgoing.at[me], blocks.at[:, rows_of(me), :], own)
    keep.start()
    met(devices - 1 + len(across))
    def send_all(order, _):
        for near in range(group):
            copy_at(far_of(order), near).start()
        return 0

    lax.fori_loop(0, ring - 1, send_all, 0)
    for near in range(1, group):
        copy_at(0, near).start()
    keep.wait()
    part[...] = jnp.zeros_like(part)

    def add(order, _):
        far = far_of(order)
        for near in range(group):

            @pl.when(far * group + near > 0)
            def _(near=near):
                copy_at(far, near).wait_recv()

        for there in range(tall):
            source = (there * ring + (turn - far + ring) % ring) * cores
            rows = pl.ds(pl.multiple_of(source * sub_rows, sub_rows * cores), sub_rows * cores)
            high, low = halves(jnp.concatenate([blocks[0, rows, :], blocks[1, rows, :]], axis=1))

            def one(x, y):
                return lax.dot_general(x, y, (((0,), (0,)), ((), ())), preferred_element_type=F32)

            main, side_part = one(high, high), one(high, low)
            whole = main + (side_part + side_part.T)
            part[:block, :] += whole[:block, :block]
            part[block : 2 * block, :] += whole[:block, block:]
            part[2 * block :, :] += whole[block:, block:]
        return 0

    lax.fori_loop(0, ring, add, 0)
    position, first, last, _, _ = pair_place()

    def raws():
        return raw_copies(blocks, before, after, raw_send, raw_recv, position)

    both_ways(*raws(), first, last, lambda copy: copy.start())
    row_total(grid, GRAM_STREAMS, part, total, slots, sums, sum_send, sum_recv)
    gram[:block, :block] = total[:block, :]
    gram[:block, block:] = total[block : 2 * block, :]
    gram[block:, :block] = total[block : 2 * block, :].T
    gram[block:, block:] = total[2 * block :, :]

    both_arrive(*raws(), first, last)
    both_ways(*raws(), first, last, lambda copy: copy.wait_send())

    def sent(step, _):
        copy_at(step // group, step % group).wait_send()
        return 0

    lax.fori_loop(1, devices, sent, 0)


def deal(picked, grid, cut):
    devices, _, sub_rows, block = picked.shape
    return pl.pallas_call(
        functools.partial(deal_kernel, grid, cut),
        out_shape=(
            jax.ShapeDtypeStruct((2, sub_rows * devices, block), F32),
            jax.ShapeDtypeStruct((2 * block, 2 * block), F32),
            raw_shape(DEAL_AHEAD, block),
            raw_shape(DEAL_AHEAD, block),
        ),
        in_specs=[VMEM],
        out_specs=(VMEM,) * 4,
        scratch_shapes=[
            pltpu.SemaphoreType.DMA((devices,)),
            pltpu.SemaphoreType.DMA((devices,)),
            pltpu.SemaphoreType.DMA,
            pltpu.SemaphoreType.DMA((2,)),
            pltpu.SemaphoreType.DMA((2,)),
        ]
        + total_scratch(grid, GRAM_STREAMS, 3 * block, block),
        compiler_params=pltpu.CompilerParams(collective_id=0, has_side_effects=True, vmem_limit_bytes=GRANT),
        name="deal",
    )(picked)


def join_kernel(blocks, joined, sems):
    block = blocks.shape[2]
    parts = sems.shape[1]
    rows = blocks.shape[1] // parts
    copies = []
    for half in range(2):
        for part in range(parts):
            here = pl.ds(part * rows, rows)
            copies.append(
                pltpu.make_async_copy(
                    blocks.at[half, here], joined.at[here, pl.ds(half * block, block)], sems.at[half, part]
                )
            )
            copies[-1].start()
    for copy in copies:
        copy.wait()


def join(blocks):
    _, rows, block = blocks.shape
    return pl.pallas_call(
        join_kernel,
        out_shape=jax.ShapeDtypeStruct((rows, 2 * block), F32),
        in_specs=[pl.BlockSpec(memory_space=pl.ANY)],
        out_specs=pl.BlockSpec(memory_space=pltpu.HBM),
        scratch_shapes=[pltpu.SemaphoreType.DMA((2, 4))],
        compiler_params=pltpu.CompilerParams(vmem_limit_bytes=GRANT),
        name="join",
    )(blocks)


def cuts():
    grids = {16: (4, 4), 4: (2, 2)}
    pairs = {32: (2, 8, 2), 4: (1, 2, 2)}
    return grids[lax.axis_size("row")], pairs[lax.axis_size("pair")]


def body(embedding, pairing):
    grid, cut = cuts()
    blocks, gram, before, after = deal(pick(embedding, pairing), grid, cut)
    total_rows = blocks.shape[1] * lax.axis_size("row")
    for round_num in range(ROUNDS):
        rotation, upper_gram, lower_gram = make_rotation(gram, total_rows)
        if round_num + 1 < ROUNDS:
            blocks, gram, before, after = next_round(
                blocks, before, after, rotation, upper_gram, lower_gram, grid, 2 + round_num
            )
        else:
            blocks = last_round(blocks, before, after, rotation)
    return join(blocks)


def solution(mesh):
    in_specs = (P(("row", "pair"), None), P())
    out_specs = P("row", "pair")
    return jax.shard_map(body, mesh=mesh, in_specs=in_specs, out_specs=out_specs, check_vma=False)
```

```python
import functools

import jax
import jax.numpy as jnp
from jax import lax
from jax.experimental import pallas as pl
from jax.experimental.pallas import tpu as pltpu
from jax.sharding import PartitionSpec as P

ROUNDS = 3
SWEEPS = 2
F32 = jnp.float32
BF16 = jnp.bfloat16


def halves(a):
    high = a.astype(BF16)
    return high, (a - high.astype(F32)).astype(BF16)


def product(a, b, dims=((1,), (0,))):
    def one(x, y):
        return lax.dot_general(x, y, (dims, ((), ())), preferred_element_type=F32)

    a_high, a_low = a
    b_high, b_low = b
    return one(a_high, b_high) + (one(a_high, b_low) + one(a_low, b_high))


def rotation_kernel(total_rows, gram_ref, rotation_ref, upper_ref, lower_ref, current, basis, level, strict):
    width = gram_ref.shape[0]
    block = width // 2
    rows = lax.broadcasted_iota(jnp.int32, (width, width), 0)
    cols = lax.broadcasted_iota(jnp.int32, (width, width), 1)
    eye = rows == cols
    above = rows < cols

    def diag_row(a):
        return jnp.sum(jnp.where(eye, a, 0.0), axis=0, keepdims=True)

    def diag_col(a):
        return jnp.sum(jnp.where(eye, a, 0.0), axis=1, keepdims=True)

    current[...] = gram_ref[...]
    for sweep in range(SWEEPS):
        scaled = current[...] * (1.0 / total_rows)
        level_row = diag_row(scaled) + 1e-06
        level_col = diag_col(scaled) + 1e-06
        spread = level_row - level_col
        generator = scaled * spread / (spread * spread + 0.25 * level_col * level_row)
        parts = halves(generator)
        square = product(parts, parts)
        basis[...] = jnp.where(eye, 1.0, 0.0) + generator
        level[...] = 1.0 - diag_col(square)
        strict[...] = jnp.where(above, -square, 0.0)
        size = jnp.sum(square * square * jnp.where(above, 1.0, 0.0))

        @pl.when(size > 0.0625)
        def _():
            exact = jnp.dot(generator, generator, precision=lax.Precision.HIGHEST, preferred_element_type=F32)
            current_metric = jnp.where(eye, 1.0, 0.0) - exact
            strict[...] = 0.5 * (current_metric + current_metric.T)

            def step(k, _):
                pivot_row = strict[pl.ds(k, 1), :]
                lane = lax.broadcasted_iota(jnp.int32, (1, width), 1)
                pivot = jnp.sum(jnp.where(lane == k, pivot_row, 0.0), axis=1, keepdims=True)
                after = jnp.where(lane > k, pivot_row / pivot, 0.0)
                metric = strict[...]
                pivot_col = jnp.sum(jnp.where(cols == k, metric, 0.0), axis=1, keepdims=True)
                strict[...] = metric - pivot_col * after
                turned = basis[...]
                basis_col = jnp.sum(jnp.where(cols == k, turned, 0.0), axis=1, keepdims=True)
                basis[...] = turned - basis_col * after
                return 0

            lax.fori_loop(0, width, step, 0)
            level[...] = diag_col(strict[...])
            strict[...] = jnp.zeros_like(strict)

        def eliminate(state):
            _, count = state
            upper = strict[...]
            scale = level[...]
            ratio = upper / scale
            ratio_parts = halves(ratio)
            turned = basis[...]
            basis[...] = turned - product(halves(turned), ratio_parts)
            size_now = jnp.sum(upper * upper)

            @pl.when(size_now > 1e-06)
            def _():
                second = product(halves(upper), ratio_parts)
                mixed = product(halves(ratio.T), halves(0.5 * upper - second))
                level[...] = scale - 2.0 * diag_col(mixed)
                strict[...] = jnp.where(above, -(second + mixed + mixed.T), 0.0)

            return size_now, count + 1

        lax.while_loop(
            lambda state: jnp.logical_and(state[0] > 1e-06, state[1] < width),
            eliminate,
            (jnp.float32(1.0), jnp.int32(0)),
        )
        level_out = jnp.sum(jnp.where(eye, jnp.broadcast_to(level[...], (width, width)), 0.0), axis=0, keepdims=True)
        step_rot = basis[...] * lax.rsqrt(level_out)
        step_parts = halves(step_rot)
        half = product(halves(current[...]), step_parts)
        if sweep == 0:
            rotation_ref[...] = step_rot
        else:
            rotation_ref[...] = product(halves(rotation_ref[...]), step_parts)
        if sweep + 1 < SWEEPS:
            current[...] = product(halves(step_rot.T), halves(half))
        else:
            turned_t = step_rot.T
            upper_ref[...] = product(halves(turned_t[:block]), halves(half[:, :block]))
            lower_ref[...] = product(halves(turned_t[block:]), halves(half[:, block:]))


def make_rotation(gram, total_rows):
    width = gram.shape[0]
    block = width // 2
    return pl.pallas_call(
        functools.partial(rotation_kernel, total_rows),
        out_shape=(
            jax.ShapeDtypeStruct((width, width), F32),
            jax.ShapeDtypeStruct((block, block), F32),
            jax.ShapeDtypeStruct((block, block), F32),
        ),
        in_specs=[pl.BlockSpec(memory_space=pltpu.VMEM)],
        out_specs=(pl.BlockSpec(memory_space=pltpu.VMEM),) * 3,
        scratch_shapes=[
            pltpu.VMEM((width, width), F32),
            pltpu.VMEM((width, width), F32),
            pltpu.VMEM((width, 1), F32),
            pltpu.VMEM((width, width), F32),
        ],
        compiler_params=pltpu.CompilerParams(vmem_limit_bytes=14 * 2**20),
        name="rotation",
    )(gram)


MESH = pl.DeviceIdType.MESH
CHUNK = 256
GRAM_STREAMS = 3
CROSS_STREAMS = 2
DEAL_AHEAD = 5
ROUND_AHEAD = 3
GRANT = 20 * 2**20


def greet(peers):
    barrier = pltpu.get_barrier_semaphore()
    for peer, wanted in peers:
        if wanted is None:
            pl.semaphore_signal(barrier, inc=1, device_id=peer, device_id_type=MESH)
        else:

            @pl.when(wanted)
            def _(peer=peer):
                pl.semaphore_signal(barrier, inc=1, device_id=peer, device_id_type=MESH)


def met(count):
    pl.semaphore_wait(pltpu.get_barrier_semaphore(), count)


def row_place(grid):
    deep, wide = grid
    me = lax.axis_index("row")
    return me // wide, me % wide


def row_peers(grid):
    deep, wide = grid
    down, across = row_place(grid)
    peers = [({"row": down * wide + (across + j) % wide}, None) for j in range(1, wide)]
    return peers + [({"row": partner * wide + across}, None) for partner in y_partners(deep, down)]


def y_partners(deep, down):
    assert deep == 4
    return down + 1 - 2 * (down % 2), deep - 1 - down


def row_total(grid, streams, part, total, slots, sums, send, recv, beside):
    deep, wide = grid
    down, across = row_place(grid)
    piece = part.shape[0] // (wide * streams)

    def rows_of(stream, owner):
        return pl.ds(pl.multiple_of((stream * wide + owner) * piece, 8), piece)

    def across_peer(j):
        return {"row": down * wide + (across + j) % wide}

    def scatter(stream, j):
        theirs = rows_of(stream, (across + j) % wide)
        return pltpu.make_async_remote_copy(
            part.at[theirs], slots.at[stream, j], send.at[0, stream, j], recv.at[0, stream, j], across_peer(j), MESH
        )

    def exchange(stream, step):
        peer = {"row": y_partners(deep, down)[step] * wide + across}
        return pltpu.make_async_remote_copy(
            sums.at[stream, 2 * step], sums.at[stream, 2 * step + 1], send.at[1, stream, step],
            recv.at[1, stream, step], peer, MESH,
        )

    def gather(stream, j):
        mine = total.at[rows_of(stream, across)]
        return pltpu.make_async_remote_copy(
            mine, mine, send.at[2, stream, j], recv.at[2, stream, j], across_peer(j), MESH
        )

    for stream in range(streams):
        for j in range(1, wide):
            scatter(stream, j).start()
    beside(0)
    for stream in range(streams):
        for j in range(1, wide):
            scatter(stream, j).wait_recv()
        value = part[rows_of(stream, across), :]
        for j in range(1, wide):
            value = value + slots[stream, j]
        sums[stream, 0] = value
        exchange(stream, 0).start()
    beside(1)
    for stream in range(streams):
        exchange(stream, 0).wait_recv()
        sums[stream, 2] = sums[stream, 0] + sums[stream, 1]
        exchange(stream, 1).start()
    beside(2)
    for stream in range(streams):
        exchange(stream, 1).wait_recv()
        value = sums[stream, 2] + sums[stream, 3]
        total[rows_of(stream, across), :] = value
        for j in range(1, wide):
            gather(stream, j).start()
    for stream in range(streams):
        for j in range(1, wide):
            gather(stream, j).wait_recv()
    for stream in range(streams):
        for j in range(1, wide):
            scatter(stream, j).wait_send()
            gather(stream, j).wait_send()
        for step in range(2):
            exchange(stream, step).wait_send()


def total_scratch(grid, streams, rows, block):
    deep, wide = grid
    steps = max(grid)
    piece = rows // (wide * streams)
    return [
        pltpu.VMEM((rows, block), F32),
        pltpu.VMEM((rows, block), F32),
        pltpu.VMEM((streams, wide, piece, block), F32),
        pltpu.VMEM((streams, 4, piece, block), F32),
        pltpu.SemaphoreType.DMA((3, streams, steps)),
        pltpu.SemaphoreType.DMA((3, streams, steps)),
    ]


def chunk_rows(c):
    return pl.ds(pl.multiple_of(c * CHUNK, CHUNK), CHUNK)


def both_ways(onward, backward, first, last, act):
    @pl.when(jnp.logical_not(last))
    def _():
        act(onward)

    @pl.when(jnp.logical_not(first))
    def _():
        act(backward)


def both_arrive(onward, backward, first, last):
    @pl.when(jnp.logical_not(first))
    def _():
        onward.wait_recv()

    @pl.when(jnp.logical_not(last))
    def _():
        backward.wait_recv()


def neighbour_copies(sources, targets, sends, recvs, position):
    def one(way, distance):
        return pltpu.make_async_remote_copy(
            sources[way], targets[way], sends[way], recvs[way], {"pair": position + distance}, MESH
        )

    return one(0, 1), one(1, -1)


def raw_moves(blocks, before, after, send, recv, position, first, last, span):
    pieces = 2 * (before.shape[1] // CHUNK)

    def copies(k):
        half = k % 2
        rows = chunk_rows(k // 2)
        source = blocks.at[half, rows]
        return neighbour_copies(
            (source, source),
            (before.at[half, rows], after.at[half, rows]),
            (send.at[0, k], send.at[1, k]),
            (recv.at[0, k], recv.at[1, k]),
            position,
        )

    bent_on = (position + 1) % span == 0
    bent_back = position % span == 0
    cuts_at = (0, (pieces + 1) // 3, (2 * pieces + 1) // 3, pieces)

    def start(low, high, on, back):
        def one(k, _):
            onward, backward = copies(k)

            @pl.when(jnp.logical_and(jnp.logical_not(last), on))
            def _():
                onward.start()

            @pl.when(jnp.logical_and(jnp.logical_not(first), back))
            def _():
                backward.start()

            return 0

        lax.fori_loop(low, high, one, 0)

    def beside(phase):
        if phase == 0:
            start(0, pieces, jnp.logical_not(bent_on), jnp.logical_not(bent_back))
        start(cuts_at[phase], cuts_at[phase + 1], bent_on, bent_back)

    def finish():
        def one(k, _):
            both_arrive(*copies(k), first, last)
            both_ways(*copies(k), first, last, lambda copy: copy.wait_send())
            return 0

        lax.fori_loop(0, pieces, one, 0)

    return beside, finish


def turn_and_move(
    blocks, before, after, rotation, fresh, ahead, back, own_high, own_low, lent, got, got_high, got_low,
    send, recv, spin_send, spin_recv, first, last, position, count, use,
):
    block = blocks.shape[2]
    chunks = blocks.shape[1] // CHUNK
    there = before.shape[1] // CHUNK
    high, low = halves(rotation[...])
    own_high[...] = high
    own_low[...] = low
    lent[0] = jnp.where(first, rotation[:, block:], rotation[:, :block])
    lent[1] = rotation[:, block:]

    def pair_rows(source, c):
        rows = chunk_rows(c)
        return halves(jnp.concatenate([source[0, rows, :], source[1, rows, :]], axis=1))

    def copies(c):
        rows = chunk_rows(c)
        return neighbour_copies(
            (ahead.at[rows], back.at[rows]),
            (fresh.at[0, rows], fresh.at[1, rows]),
            (send.at[0, c], send.at[1, c]),
            (recv.at[0, c], recv.at[1, c]),
            position,
        )

    def spins():
        return neighbour_copies(
            (lent.at[0], lent.at[1]),
            (got.at[0], got.at[1]),
            (spin_send.at[0], spin_send.at[1]),
            (spin_recv.at[0], spin_recv.at[1]),
            position,
        )

    def turn(c, _):
        rows = chunk_rows(c)
        turned = product(pair_rows(blocks, c), (own_high[...], own_low[...]))
        upper, lower = turned[:, :block], turned[:, block:]
        ahead[rows, :] = jnp.where(first, lower, upper)
        back[rows, :] = lower

        @pl.when(first)
        def _():
            fresh[0, rows, :] = upper

        @pl.when(last)
        def _():
            fresh[1, rows, :] = upper

        return 0

    def leave(c, _):
        both_ways(*copies(c), first, last, lambda copy: copy.start())
        return 0

    def turn_and_leave(c, _):
        turn(c, 0)
        return leave(c, 0)

    early = (chunks + there) // 2
    lax.fori_loop(there, early, turn, 0)
    met(count)
    both_ways(*spins(), first, last, lambda copy: copy.start())
    lax.fori_loop(there, early, leave, 0)
    lax.fori_loop(early, chunks, turn_and_leave, 0)
    both_arrive(*spins(), first, last)

    for way, edge in ((0, first), (1, last)):

        @pl.when(edge)
        def _(way=way):
            got_high[way] = own_high[:, :block]
            got_low[way] = own_low[:, :block]

        @pl.when(jnp.logical_not(edge))
        def _(way=way):
            high, low = halves(got[way])
            got_high[way] = high
            got_low[way] = low

    def turn_there(c, _):
        rows = chunk_rows(c)
        for way, edge, raw in ((0, first, before), (1, last, after)):

            @pl.when(edge)
            def _(way=way):
                fresh[way, rows, :] = product(pair_rows(blocks, c), (got_high[way], got_low[way]))

            @pl.when(jnp.logical_not(edge))
            def _(way=way, raw=raw):
                fresh[way, rows, :] = product(pair_rows(raw, c), (got_high[way], got_low[way]))

        use(c)
        return 0

    lax.fori_loop(0, there, turn_there, 0)

    def take():
        def one(c, _):
            both_arrive(*copies(c), first, last)
            use(c)
            return 0

        lax.fori_loop(there, chunks, one, 0)

    def finish():
        both_ways(*spins(), first, last, lambda copy: copy.wait_send())

        def left(c, _):
            both_ways(*copies(c), first, last, lambda copy: copy.wait_send())
            return 0

        lax.fori_loop(there, chunks, left, 0)

    return take, finish


def pair_place():
    position = lax.axis_index("pair")
    first = position == 0
    last = position == lax.axis_size("pair") - 1
    count = jnp.where(first, 0, 1) + jnp.where(last, 0, 1)
    peers = [
        ({"pair": position + 1}, jnp.logical_not(last)),
        ({"pair": position - 1}, jnp.logical_not(first)),
    ]
    return position, first, last, peers, count


def round_kernel(
    grid, span, blocks, before, after, rotation, upper_gram, lower_gram, fresh, gram, next_before, next_after,
    ahead, back, own_high, own_low, lent, got, got_high, got_low, send, recv, spin_send, spin_recv,
    ahead_gram, back_gram, gram_send, gram_recv, raw_send, raw_recv,
    part, total, slots, sums, sum_send, sum_recv,
):
    position, first, last, peers, count = pair_place()
    block = blocks.shape[2]
    across = row_peers(grid)
    greet(peers + across)
    ahead_gram[...] = jnp.where(first, lower_gram[...], upper_gram[...])
    back_gram[...] = lower_gram[...]

    @pl.when(first)
    def _():
        gram[:block, :block] = upper_gram[...]

    @pl.when(last)
    def _():
        gram[block:, block:] = upper_gram[...]

    part[...] = jnp.zeros_like(part)

    def cross(c):
        rows = chunk_rows(c)
        part[...] += product(halves(fresh[0, rows, :]), halves(fresh[1, rows, :]), ((0,), (0,)))

    take, finish = turn_and_move(
        blocks, before, after, rotation, fresh, ahead, back, own_high, own_low, lent, got, got_high, got_low,
        send, recv, spin_send, spin_recv, first, last, position, count + len(across), cross,
    )

    def grams():
        return neighbour_copies(
            (ahead_gram, back_gram),
            (gram.at[pl.ds(0, block), pl.ds(0, block)], gram.at[pl.ds(block, block), pl.ds(block, block)]),
            (gram_send.at[0], gram_send.at[1]),
            (gram_recv.at[0], gram_recv.at[1]),
            position,
        )

    beside, raws_finish = raw_moves(
        fresh, next_before, next_after, raw_send, raw_recv, position, first, last, span
    )
    both_ways(*grams(), first, last, lambda copy: copy.start())
    take()
    row_total(grid, CROSS_STREAMS, part, total, slots, sums, sum_send, sum_recv, beside)
    gram[:block, block:] = total[...]
    gram[block:, :block] = total[...].T
    both_arrive(*grams(), first, last)
    both_ways(*grams(), first, last, lambda copy: copy.wait_send())
    raws_finish()
    finish()


def last_kernel(
    blocks, before, after, rotation, fresh,
    ahead, back, own_high, own_low, lent, got, got_high, got_low, send, recv, spin_send, spin_recv,
):
    position, first, last, peers, count = pair_place()
    greet(peers)
    take, finish = turn_and_move(
        blocks, before, after, rotation, fresh, ahead, back, own_high, own_low, lent, got, got_high, got_low,
        send, recv, spin_send, spin_recv, first, last, position, count, lambda c: None,
    )
    take()
    finish()


def move_scratch(rows, block):
    width = 2 * block
    chunks = rows // CHUNK
    return [
        pltpu.VMEM((rows, block), F32),
        pltpu.VMEM((rows, block), F32),
        pltpu.VMEM((width, width), BF16),
        pltpu.VMEM((width, width), BF16),
        pltpu.VMEM((2, width, block), F32),
        pltpu.VMEM((2, width, block), F32),
        pltpu.VMEM((2, width, block), BF16),
        pltpu.VMEM((2, width, block), BF16),
        pltpu.SemaphoreType.DMA((2, chunks)),
        pltpu.SemaphoreType.DMA((2, chunks)),
        pltpu.SemaphoreType.DMA((2,)),
        pltpu.SemaphoreType.DMA((2,)),
    ]


VMEM = pl.BlockSpec(memory_space=pltpu.VMEM)


def raw_shape(chunks, block):
    return jax.ShapeDtypeStruct((2, chunks * CHUNK, block), F32)


def next_round(blocks, before, after, rotation, upper_gram, lower_gram, grid, span, collective):
    _, rows, block = blocks.shape
    return pl.pallas_call(
        functools.partial(round_kernel, grid, span),
        out_shape=(
            jax.ShapeDtypeStruct(blocks.shape, F32),
            jax.ShapeDtypeStruct((2 * block, 2 * block), F32),
            raw_shape(ROUND_AHEAD, block),
            raw_shape(ROUND_AHEAD, block),
        ),
        in_specs=[VMEM] * 6,
        out_specs=(VMEM,) * 4,
        scratch_shapes=move_scratch(rows, block)
        + [pltpu.VMEM((block, block), F32), pltpu.VMEM((block, block), F32)]
        + [pltpu.SemaphoreType.DMA((2,))] * 2
        + [pltpu.SemaphoreType.DMA((2, 2 * ROUND_AHEAD))] * 2
        + total_scratch(grid, CROSS_STREAMS, block, block),
        compiler_params=pltpu.CompilerParams(
            collective_id=collective, has_side_effects=True, vmem_limit_bytes=GRANT
        ),
        name="next_round",
    )(blocks, before, after, rotation, upper_gram, lower_gram)


def last_round(blocks, before, after, rotation):
    _, rows, block = blocks.shape
    return pl.pallas_call(
        last_kernel,
        out_shape=jax.ShapeDtypeStruct(blocks.shape, F32),
        in_specs=[VMEM] * 4,
        out_specs=VMEM,
        scratch_shapes=move_scratch(rows, block),
        compiler_params=pltpu.CompilerParams(collective_id=1, has_side_effects=True, vmem_limit_bytes=GRANT),
        name="last_round",
    )(blocks, before, after, rotation)


def pick_kernel(embedding, pairing, picked):
    block = picked.shape[3]

    def one(target, _):
        for half in range(2):
            source = pl.multiple_of(pairing[2 * target + half] * block, block)
            picked[target, half] = embedding[:, pl.ds(source, block)]
        return 0

    lax.fori_loop(0, picked.shape[0], one, 0, unroll=4)


def pick(embedding, pairing):
    sub_rows, columns = embedding.shape
    slots = pairing.shape[0]
    return pl.pallas_call(
        pick_kernel,
        out_shape=jax.ShapeDtypeStruct((slots // 2, 2, sub_rows, columns // slots), F32),
        in_specs=[VMEM, pl.BlockSpec(memory_space=pltpu.SMEM)],
        out_specs=VMEM,
        compiler_params=pltpu.CompilerParams(vmem_limit_bytes=GRANT),
        name="pick",
    )(embedding, pairing)


def deal_kernel(
    grid, cut, outgoing, blocks, gram, before, after, send, recv, own, raw_send, raw_recv,
    part, total, slots, sums, sum_send, sum_recv,
):
    tall, ring, cores = cut
    sub_rows = outgoing.shape[2]
    block = blocks.shape[2]
    devices = lax.axis_size("pair")
    me = lax.axis_index("pair")
    core, turn, side = me % cores, me // cores % ring, me // (cores * ring)
    halfway = ring // 2
    group = tall * cores

    def device(there_side, there_turn, there_core):
        return (there_side % tall * ring + (there_turn + 2 * ring) % ring) * cores + there_core % cores

    def target_of(far, near):
        return device(side + near // cores, turn + far, core + near % cores)

    def rows_of(index):
        return pl.ds(pl.multiple_of(index * sub_rows, sub_rows), sub_rows)

    def far_of(order):
        away = (order + 1) // 2
        return halfway + away - 2 * away * (order % 2)

    def copy_at(far, near):
        target = target_of(far, near)
        step = far * group + near
        return pltpu.make_async_remote_copy(
            outgoing.at[target], blocks.at[:, rows_of(me), :], send.at[step], recv.at[step], {"pair": target}, MESH
        )

    barrier = pltpu.get_barrier_semaphore()

    def call(step, _):
        target = target_of(step // group, step % group)
        pl.semaphore_signal(barrier, inc=1, device_id={"pair": target}, device_id_type=MESH)
        return 0

    lax.fori_loop(1, devices, call, 0)
    across = row_peers(grid)
    greet(across)
    keep = pltpu.make_async_copy(outgoing.at[me], blocks.at[:, rows_of(me), :], own)
    keep.start()
    met(devices - 1 + len(across))
    def send_all(order, _):
        for near in range(group):
            copy_at(far_of(order), near).start()
        return 0

    lax.fori_loop(0, ring - 1, send_all, 0)
    for near in range(1, group):
        copy_at(0, near).start()
    keep.wait()
    part[...] = jnp.zeros_like(part)

    def add(order, _):
        far = far_of(order)
        for near in range(group):

            @pl.when(far * group + near > 0)
            def _(near=near):
                copy_at(far, near).wait_recv()

        for there in range(tall):
            source = (there * ring + (turn - far + ring) % ring) * cores
            rows = pl.ds(pl.multiple_of(source * sub_rows, sub_rows * cores), sub_rows * cores)
            high, low = halves(jnp.concatenate([blocks[0, rows, :], blocks[1, rows, :]], axis=1))

            def one(x, y):
                return lax.dot_general(x, y, (((0,), (0,)), ((), ())), preferred_element_type=F32)

            main, side_part = one(high, high), one(high, low)
            whole = main + (side_part + side_part.T)
            part[:block, :] += whole[:block, :block]
            part[block : 2 * block, :] += whole[:block, block:]
            part[2 * block :, :] += whole[block:, block:]
        return 0

    lax.fori_loop(0, ring, add, 0)
    position, first, last, _, _ = pair_place()

    beside, raws_finish = raw_moves(
        blocks, before, after, raw_send, raw_recv, position, first, last, ring * cores
    )
    row_total(grid, GRAM_STREAMS, part, total, slots, sums, sum_send, sum_recv, beside)
    gram[:block, :block] = total[:block, :]
    gram[:block, block:] = total[block : 2 * block, :]
    gram[block:, :block] = total[block : 2 * block, :].T
    gram[block:, block:] = total[2 * block :, :]

    raws_finish()

    def sent(step, _):
        copy_at(step // group, step % group).wait_send()
        return 0

    lax.fori_loop(1, devices, sent, 0)


def deal(picked, grid, cut):
    devices, _, sub_rows, block = picked.shape
    return pl.pallas_call(
        functools.partial(deal_kernel, grid, cut),
        out_shape=(
            jax.ShapeDtypeStruct((2, sub_rows * devices, block), F32),
            jax.ShapeDtypeStruct((2 * block, 2 * block), F32),
            raw_shape(DEAL_AHEAD, block),
            raw_shape(DEAL_AHEAD, block),
        ),
        in_specs=[VMEM],
        out_specs=(VMEM,) * 4,
        scratch_shapes=[
            pltpu.SemaphoreType.DMA((devices,)),
            pltpu.SemaphoreType.DMA((devices,)),
            pltpu.SemaphoreType.DMA,
            pltpu.SemaphoreType.DMA((2, 2 * DEAL_AHEAD)),
            pltpu.SemaphoreType.DMA((2, 2 * DEAL_AHEAD)),
        ]
        + total_scratch(grid, GRAM_STREAMS, 3 * block, block),
        compiler_params=pltpu.CompilerParams(collective_id=0, has_side_effects=True, vmem_limit_bytes=GRANT),
        name="deal",
    )(picked)


def join_kernel(blocks, joined, sems):
    block = blocks.shape[2]
    parts = sems.shape[1]
    rows = blocks.shape[1] // parts
    copies = []
    for half in range(2):
        for part in range(parts):
            here = pl.ds(part * rows, rows)
            copies.append(
                pltpu.make_async_copy(
                    blocks.at[half, here], joined.at[here, pl.ds(half * block, block)], sems.at[half, part]
                )
            )
            copies[-1].start()
    for copy in copies:
        copy.wait()


def join(blocks):
    _, rows, block = blocks.shape
    return pl.pallas_call(
        join_kernel,
        out_shape=jax.ShapeDtypeStruct((rows, 2 * block), F32),
        in_specs=[pl.BlockSpec(memory_space=pl.ANY)],
        out_specs=pl.BlockSpec(memory_space=pltpu.HBM),
        scratch_shapes=[pltpu.SemaphoreType.DMA((2, 4))],
        compiler_params=pltpu.CompilerParams(vmem_limit_bytes=GRANT),
        name="join",
    )(blocks)


def cuts():
    grids = {16: (4, 4), 4: (2, 2)}
    pairs = {32: (2, 8, 2), 4: (1, 2, 2)}
    return grids[lax.axis_size("row")], pairs[lax.axis_size("pair")]


def body(embedding, pairing):
    grid, cut = cuts()
    blocks, gram, before, after = deal(pick(embedding, pairing), grid, cut)
    total_rows = blocks.shape[1] * lax.axis_size("row")
    for round_num in range(ROUNDS):
        rotation, upper_gram, lower_gram = make_rotation(gram, total_rows)
        if round_num + 1 < ROUNDS:
            blocks, gram, before, after = next_round(
                blocks, before, after, rotation, upper_gram, lower_gram, grid, cut[1] * cut[2], 2 + round_num
            )
        else:
            blocks = last_round(blocks, before, after, rotation)
    return join(blocks)


def solution(mesh):
    in_specs = (P(("row", "pair"), None), P())
    out_specs = P("row", "pair")
    return jax.shard_map(body, mesh=mesh, in_specs=in_specs, out_specs=out_specs, check_vma=False)
```

```python
import functools

import jax
import jax.numpy as jnp
from jax import lax
from jax.experimental import pallas as pl
from jax.experimental.pallas import tpu as pltpu
from jax.sharding import PartitionSpec as P

ROUNDS = 3
SWEEPS = 2
F32 = jnp.float32
BF16 = jnp.bfloat16


def halves(a):
    high = a.astype(BF16)
    return high, (a - high.astype(F32)).astype(BF16)


def product(a, b, dims=((1,), (0,))):
    def one(x, y):
        return lax.dot_general(x, y, (dims, ((), ())), preferred_element_type=F32)

    a_high, a_low = a
    b_high, b_low = b
    return one(a_high, b_high) + (one(a_high, b_low) + one(a_low, b_high))


def rotation_kernel(total_rows, gram_ref, rotation_ref, upper_ref, lower_ref, current, basis, level, strict):
    width = gram_ref.shape[0]
    block = width // 2
    rows = lax.broadcasted_iota(jnp.int32, (width, width), 0)
    cols = lax.broadcasted_iota(jnp.int32, (width, width), 1)
    eye = rows == cols
    above = rows < cols

    small_eye = eye[:block, :block]

    def diag(a, axis):
        corners = (a[:block, :block], a[block:, block:])
        return jnp.concatenate(
            [jnp.sum(jnp.where(small_eye, corner, 0.0), axis=axis, keepdims=True) for corner in corners], axis=1 - axis
        )

    def diag_row(a):
        return diag(a, 0)

    def diag_col(a):
        return diag(a, 1)

    current[...] = gram_ref[...]
    for sweep in range(SWEEPS):
        scaled = current[...] * (1.0 / total_rows)
        level_row = diag_row(scaled) + 1e-06
        level_col = diag_col(scaled) + 1e-06
        spread = level_row - level_col
        generator = scaled * spread / (spread * spread + 0.25 * level_col * level_row)
        parts = halves(generator)
        square = product(parts, parts)
        basis[...] = jnp.where(eye, 1.0, 0.0) + generator
        level[...] = 1.0 - diag_col(square)
        first_strict = jnp.where(above, -square, 0.0)
        strict[...] = first_strict
        size = jnp.sum(first_strict * first_strict)

        @pl.when(size > 0.0625)
        def _():
            exact = jnp.dot(generator, generator, precision=lax.Precision.HIGHEST, preferred_element_type=F32)
            current_metric = jnp.where(eye, 1.0, 0.0) - exact
            strict[...] = 0.5 * (current_metric + current_metric.T)

            def step(k, _):
                pivot_row = strict[pl.ds(k, 1), :]
                lane = lax.broadcasted_iota(jnp.int32, (1, width), 1)
                pivot = jnp.sum(jnp.where(lane == k, pivot_row, 0.0), axis=1, keepdims=True)
                after = jnp.where(lane > k, pivot_row / pivot, 0.0)
                metric = strict[...]
                pivot_col = jnp.sum(jnp.where(cols == k, metric, 0.0), axis=1, keepdims=True)
                strict[...] = metric - pivot_col * after
                turned = basis[...]
                basis_col = jnp.sum(jnp.where(cols == k, turned, 0.0), axis=1, keepdims=True)
                basis[...] = turned - basis_col * after
                return 0

            lax.fori_loop(0, width, step, 0)
            level[...] = diag_col(strict[...])
            strict[...] = jnp.zeros_like(strict)

        def eliminate(state):
            _, count = state
            upper = strict[...]
            scale = level[...]
            ratio = upper * (1.0 / scale)
            turned = basis[...]
            both = product(halves(jnp.concatenate([turned, upper], axis=0)), halves(ratio))
            basis[...] = turned - both[:width]
            second = both[width:]
            mixed = product(halves(ratio.T), halves(0.5 * upper - second))
            level[...] = scale - 2.0 * diag_col(mixed)
            left = jnp.where(above, -(second + mixed + mixed.T), 0.0)
            strict[...] = left
            return jnp.sum(left * left), count + 1

        lax.while_loop(
            lambda state: jnp.logical_and(state[0] > 1e-06, state[1] < width),
            eliminate,
            (jnp.where(size > 0.0625, 0.0, size), jnp.int32(0)),
        )
        turned = basis[...]
        basis[...] = turned - product(halves(turned), halves(strict[...] * (1.0 / level[...])))
        level_out = diag_row(jnp.broadcast_to(level[...], (width, width)))
        step_rot = basis[...] * lax.rsqrt(level_out)
        step_parts = halves(step_rot)
        half = product(halves(current[...]), step_parts)
        if sweep == 0:
            rotation_ref[...] = step_rot
        else:
            rotation_ref[...] = product(halves(rotation_ref[...]), step_parts)
        if sweep + 1 < SWEEPS:
            current[...] = product(halves(step_rot.T), halves(half))
        else:
            turned_t = step_rot.T
            upper_ref[...] = product(halves(turned_t[:block]), halves(half[:, :block]))
            lower_ref[...] = product(halves(turned_t[block:]), halves(half[:, block:]))


def make_rotation(gram, total_rows):
    width = gram.shape[0]
    block = width // 2
    return pl.pallas_call(
        functools.partial(rotation_kernel, total_rows),
        out_shape=(
            jax.ShapeDtypeStruct((width, width), F32),
            jax.ShapeDtypeStruct((block, block), F32),
            jax.ShapeDtypeStruct((block, block), F32),
        ),
        in_specs=[pl.BlockSpec(memory_space=pltpu.VMEM)],
        out_specs=(pl.BlockSpec(memory_space=pltpu.VMEM),) * 3,
        scratch_shapes=[
            pltpu.VMEM((width, width), F32),
            pltpu.VMEM((width, width), F32),
            pltpu.VMEM((width, 1), F32),
            pltpu.VMEM((width, width), F32),
        ],
        compiler_params=pltpu.CompilerParams(vmem_limit_bytes=14 * 2**20),
        name="rotation",
    )(gram)


MESH = pl.DeviceIdType.MESH
CHUNK = 256
GRAM_STREAMS = 3
CROSS_STREAMS = 2
DEAL_AHEAD = 5
ROUND_AHEAD = 3
GRANT = 20 * 2**20


def greet(peers):
    barrier = pltpu.get_barrier_semaphore()
    for peer, wanted in peers:
        if wanted is None:
            pl.semaphore_signal(barrier, inc=1, device_id=peer, device_id_type=MESH)
        else:

            @pl.when(wanted)
            def _(peer=peer):
                pl.semaphore_signal(barrier, inc=1, device_id=peer, device_id_type=MESH)


def met(count):
    pl.semaphore_wait(pltpu.get_barrier_semaphore(), count)


def row_place(grid):
    deep, wide = grid
    me = lax.axis_index("row")
    return me // wide, me % wide


def row_peers(grid):
    deep, wide = grid
    down, across = row_place(grid)
    peers = [({"row": down * wide + (across + j) % wide}, None) for j in range(1, wide)]
    return peers + [({"row": partner * wide + across}, None) for partner in y_partners(deep, down)]


def y_partners(deep, down):
    assert deep == 4
    return down + 1 - 2 * (down % 2), deep - 1 - down


def row_total(grid, streams, part, total, slots, sums, send, recv, beside):
    deep, wide = grid
    down, across = row_place(grid)
    piece = part.shape[0] // (wide * streams)

    def rows_of(stream, owner):
        return pl.ds(pl.multiple_of((stream * wide + owner) * piece, 8), piece)

    def across_peer(j):
        return {"row": down * wide + (across + j) % wide}

    def scatter(stream, j):
        theirs = rows_of(stream, (across + j) % wide)
        return pltpu.make_async_remote_copy(
            part.at[theirs], slots.at[stream, j], send.at[0, stream, j], recv.at[0, stream, j], across_peer(j), MESH
        )

    def exchange(stream, step):
        peer = {"row": y_partners(deep, down)[step] * wide + across}
        return pltpu.make_async_remote_copy(
            sums.at[stream, 2 * step], sums.at[stream, 2 * step + 1], send.at[1, stream, step],
            recv.at[1, stream, step], peer, MESH,
        )

    def gather(stream, j):
        mine = total.at[rows_of(stream, across)]
        return pltpu.make_async_remote_copy(
            mine, mine, send.at[2, stream, j], recv.at[2, stream, j], across_peer(j), MESH
        )

    for stream in range(streams):
        for j in range(1, wide):
            scatter(stream, j).start()
    beside(0)
    for stream in range(streams):
        for j in range(1, wide):
            scatter(stream, j).wait_recv()
        value = part[rows_of(stream, across), :]
        for j in range(1, wide):
            value = value + slots[stream, j]
        sums[stream, 0] = value
        exchange(stream, 0).start()
    beside(1)
    for stream in range(streams):
        exchange(stream, 0).wait_recv()
        sums[stream, 2] = sums[stream, 0] + sums[stream, 1]
        exchange(stream, 1).start()
    beside(2)
    for stream in range(streams):
        exchange(stream, 1).wait_recv()
        value = sums[stream, 2] + sums[stream, 3]
        total[rows_of(stream, across), :] = value
        for j in range(1, wide):
            gather(stream, j).start()
    for stream in range(streams):
        for j in range(1, wide):
            gather(stream, j).wait_recv()
    for stream in range(streams):
        for j in range(1, wide):
            scatter(stream, j).wait_send()
            gather(stream, j).wait_send()
        for step in range(2):
            exchange(stream, step).wait_send()


def total_scratch(grid, streams, rows, block):
    deep, wide = grid
    steps = max(grid)
    piece = rows // (wide * streams)
    return [
        pltpu.VMEM((rows, block), F32),
        pltpu.VMEM((rows, block), F32),
        pltpu.VMEM((streams, wide, piece, block), F32),
        pltpu.VMEM((streams, 4, piece, block), F32),
        pltpu.SemaphoreType.DMA((3, streams, steps)),
        pltpu.SemaphoreType.DMA((3, streams, steps)),
    ]


def chunk_rows(c):
    return pl.ds(pl.multiple_of(c * CHUNK, CHUNK), CHUNK)


def both_ways(onward, backward, first, last, act):
    @pl.when(jnp.logical_not(last))
    def _():
        act(onward)

    @pl.when(jnp.logical_not(first))
    def _():
        act(backward)


def both_arrive(onward, backward, first, last):
    @pl.when(jnp.logical_not(first))
    def _():
        onward.wait_recv()

    @pl.when(jnp.logical_not(last))
    def _():
        backward.wait_recv()


def neighbour_copies(sources, targets, sends, recvs, position):
    def one(way, distance):
        return pltpu.make_async_remote_copy(
            sources[way], targets[way], sends[way], recvs[way], {"pair": position + distance}, MESH
        )

    return one(0, 1), one(1, -1)


def raw_moves(blocks, before, after, send, recv, position, first, last, span):
    pieces = 2 * (before.shape[1] // CHUNK)

    def copies(k):
        half = k % 2
        rows = chunk_rows(k // 2)
        source = blocks.at[half, rows]
        return neighbour_copies(
            (source, source),
            (before.at[half, rows], after.at[half, rows]),
            (send.at[0, k], send.at[1, k]),
            (recv.at[0, k], recv.at[1, k]),
            position,
        )

    bent_on = (position + 1) % span == 0
    bent_back = position % span == 0
    cuts_at = (0, (pieces + 1) // 3, (2 * pieces + 1) // 3, pieces)

    def start(low, high, on, back):
        def one(k, _):
            onward, backward = copies(k)

            @pl.when(jnp.logical_and(jnp.logical_not(last), on))
            def _():
                onward.start()

            @pl.when(jnp.logical_and(jnp.logical_not(first), back))
            def _():
                backward.start()

            return 0

        lax.fori_loop(low, high, one, 0)

    def begin():
        start(0, pieces, jnp.logical_not(bent_on), jnp.logical_not(bent_back))

    def beside(phase):
        start(cuts_at[phase], cuts_at[phase + 1], bent_on, bent_back)

    def finish():
        def one(k, _):
            both_arrive(*copies(k), first, last)
            both_ways(*copies(k), first, last, lambda copy: copy.wait_send())
            return 0

        lax.fori_loop(0, pieces, one, 0)

    return begin, beside, finish


def turn_and_move(
    blocks, before, after, rotation, fresh, ahead, back, own_high, own_low, raw_high, raw_low, lent, got, got_high, got_low,
    send, recv, spin_send, spin_recv, first, last, position, count, use,
):
    block = blocks.shape[2]
    chunks = blocks.shape[1] // CHUNK
    there = before.shape[1] // CHUNK
    high, low = halves(rotation[...])
    own_high[...] = high
    own_low[...] = low
    lent[0] = jnp.where(first, rotation[:, block:], rotation[:, :block])
    lent[1] = rotation[:, block:]

    def pair_rows(source, c):
        rows = chunk_rows(c)
        return halves(jnp.concatenate([source[0, rows, :], source[1, rows, :]], axis=1))

    def copies(c):
        rows = chunk_rows(c)
        return neighbour_copies(
            (ahead.at[rows], back.at[rows]),
            (fresh.at[0, rows], fresh.at[1, rows]),
            (send.at[0, c], send.at[1, c]),
            (recv.at[0, c], recv.at[1, c]),
            position,
        )

    def spins():
        return neighbour_copies(
            (lent.at[0], lent.at[1]),
            (got.at[0], got.at[1]),
            (spin_send.at[0], spin_send.at[1]),
            (spin_recv.at[0], spin_recv.at[1]),
            position,
        )

    def turn(c, _):
        rows = chunk_rows(c)
        turned = product(pair_rows(blocks, c), (own_high[...], own_low[...]))
        upper, lower = turned[:, :block], turned[:, block:]
        ahead[rows, :] = jnp.where(first, lower, upper)
        back[rows, :] = lower

        @pl.when(first)
        def _():
            fresh[0, rows, :] = upper

        @pl.when(last)
        def _():
            fresh[1, rows, :] = upper

        return 0

    def leave(c, _):
        both_ways(*copies(c), first, last, lambda copy: copy.start())
        return 0

    def turn_and_leave(c, _):
        turn(c, 0)
        return leave(c, 0)

    def split_there(c, _):
        rows = chunk_rows(c)
        for way, edge, raw in ((0, first, before), (1, last, after)):

            @pl.when(edge)
            def _(way=way):
                high, low = pair_rows(blocks, c)
                raw_high[way, rows, :] = high
                raw_low[way, rows, :] = low

            @pl.when(jnp.logical_not(edge))
            def _(way=way, raw=raw):
                high, low = pair_rows(raw, c)
                raw_high[way, rows, :] = high
                raw_low[way, rows, :] = low

        return 0

    early = (chunks + there) // 2
    lax.fori_loop(there, early, turn, 0)
    met(count)
    both_ways(*spins(), first, last, lambda copy: copy.start())
    lax.fori_loop(there, early, leave, 0)
    lax.fori_loop(early, chunks, turn_and_leave, 0)
    lax.fori_loop(0, there, split_there, 0)
    both_arrive(*spins(), first, last)

    for way, edge in ((0, first), (1, last)):

        @pl.when(edge)
        def _(way=way):
            got_high[way] = own_high[:, :block]
            got_low[way] = own_low[:, :block]

        @pl.when(jnp.logical_not(edge))
        def _(way=way):
            high, low = halves(got[way])
            got_high[way] = high
            got_low[way] = low

    def turn_there(c, _):
        rows = chunk_rows(c)
        for way in range(2):
            pair = raw_high[way, rows, :], raw_low[way, rows, :]
            fresh[way, rows, :] = product(pair, (got_high[way], got_low[way]))
        use(c)
        return 0

    lax.fori_loop(0, there, turn_there, 0)

    def take():
        def one(c, _):
            both_arrive(*copies(c), first, last)
            use(c)
            return 0

        lax.fori_loop(there, chunks, one, 0)

    def finish():
        both_ways(*spins(), first, last, lambda copy: copy.wait_send())

        def left(c, _):
            both_ways(*copies(c), first, last, lambda copy: copy.wait_send())
            return 0

        lax.fori_loop(there, chunks, left, 0)

    return take, finish


def pair_place():
    position = lax.axis_index("pair")
    first = position == 0
    last = position == lax.axis_size("pair") - 1
    count = jnp.where(first, 0, 1) + jnp.where(last, 0, 1)
    peers = [
        ({"pair": position + 1}, jnp.logical_not(last)),
        ({"pair": position - 1}, jnp.logical_not(first)),
    ]
    return position, first, last, peers, count


def round_kernel(
    grid, span, blocks, before, after, rotation, upper_gram, lower_gram, fresh, gram, next_before, next_after,
    ahead, back, own_high, own_low, raw_high, raw_low, lent, got, got_high, got_low, send, recv, spin_send, spin_recv,
    ahead_gram, back_gram, gram_send, gram_recv, raw_send, raw_recv,
    part, total, slots, sums, sum_send, sum_recv,
):
    position, first, last, peers, count = pair_place()
    block = blocks.shape[2]
    across = row_peers(grid)
    greet(peers + across)
    ahead_gram[...] = jnp.where(first, lower_gram[...], upper_gram[...])
    back_gram[...] = lower_gram[...]

    @pl.when(first)
    def _():
        gram[:block, :block] = upper_gram[...]

    @pl.when(last)
    def _():
        gram[block:, block:] = upper_gram[...]

    part[...] = jnp.zeros_like(part)

    def cross(c):
        rows = chunk_rows(c)
        part[...] += product(halves(fresh[0, rows, :]), halves(fresh[1, rows, :]), ((0,), (0,)))

    take, finish = turn_and_move(
        blocks, before, after, rotation, fresh, ahead, back, own_high, own_low, raw_high, raw_low, lent, got, got_high, got_low,
        send, recv, spin_send, spin_recv, first, last, position, count + len(across), cross,
    )

    def grams():
        return neighbour_copies(
            (ahead_gram, back_gram),
            (gram.at[pl.ds(0, block), pl.ds(0, block)], gram.at[pl.ds(block, block), pl.ds(block, block)]),
            (gram_send.at[0], gram_send.at[1]),
            (gram_recv.at[0], gram_recv.at[1]),
            position,
        )

    begin, beside, raws_finish = raw_moves(
        fresh, next_before, next_after, raw_send, raw_recv, position, first, last, span
    )
    both_ways(*grams(), first, last, lambda copy: copy.start())
    begin()
    take()
    row_total(grid, CROSS_STREAMS, part, total, slots, sums, sum_send, sum_recv, beside)
    gram[:block, block:] = total[...]
    gram[block:, :block] = total[...].T
    both_arrive(*grams(), first, last)
    both_ways(*grams(), first, last, lambda copy: copy.wait_send())
    raws_finish()
    finish()


def last_kernel(
    blocks, before, after, rotation, fresh,
    ahead, back, own_high, own_low, raw_high, raw_low, lent, got, got_high, got_low, send, recv, spin_send, spin_recv,
):
    position, first, last, peers, count = pair_place()
    greet(peers)
    take, finish = turn_and_move(
        blocks, before, after, rotation, fresh, ahead, back, own_high, own_low, raw_high, raw_low, lent, got, got_high, got_low,
        send, recv, spin_send, spin_recv, first, last, position, count, lambda c: None,
    )
    take()
    finish()


def move_scratch(rows, block, there):
    width = 2 * block
    chunks = rows // CHUNK
    return [
        pltpu.VMEM((rows, block), F32),
        pltpu.VMEM((rows, block), F32),
        pltpu.VMEM((width, width), BF16),
        pltpu.VMEM((width, width), BF16),
        pltpu.VMEM((2, there, width), BF16),
        pltpu.VMEM((2, there, width), BF16),
        pltpu.VMEM((2, width, block), F32),
        pltpu.VMEM((2, width, block), F32),
        pltpu.VMEM((2, width, block), BF16),
        pltpu.VMEM((2, width, block), BF16),
        pltpu.SemaphoreType.DMA((2, chunks)),
        pltpu.SemaphoreType.DMA((2, chunks)),
        pltpu.SemaphoreType.DMA((2,)),
        pltpu.SemaphoreType.DMA((2,)),
    ]


VMEM = pl.BlockSpec(memory_space=pltpu.VMEM)


def raw_shape(chunks, block):
    return jax.ShapeDtypeStruct((2, chunks * CHUNK, block), F32)


def next_round(blocks, before, after, rotation, upper_gram, lower_gram, grid, span, collective):
    _, rows, block = blocks.shape
    return pl.pallas_call(
        functools.partial(round_kernel, grid, span),
        out_shape=(
            jax.ShapeDtypeStruct(blocks.shape, F32),
            jax.ShapeDtypeStruct((2 * block, 2 * block), F32),
            raw_shape(ROUND_AHEAD, block),
            raw_shape(ROUND_AHEAD, block),
        ),
        in_specs=[VMEM] * 6,
        out_specs=(VMEM,) * 4,
        scratch_shapes=move_scratch(rows, block, before.shape[1])
        + [pltpu.VMEM((block, block), F32), pltpu.VMEM((block, block), F32)]
        + [pltpu.SemaphoreType.DMA((2,))] * 2
        + [pltpu.SemaphoreType.DMA((2, 2 * ROUND_AHEAD))] * 2
        + total_scratch(grid, CROSS_STREAMS, block, block),
        compiler_params=pltpu.CompilerParams(
            collective_id=collective, has_side_effects=True, vmem_limit_bytes=GRANT
        ),
        name="next_round",
    )(blocks, before, after, rotation, upper_gram, lower_gram)


def last_round(blocks, before, after, rotation):
    _, rows, block = blocks.shape
    return pl.pallas_call(
        last_kernel,
        out_shape=jax.ShapeDtypeStruct(blocks.shape, F32),
        in_specs=[VMEM] * 4,
        out_specs=VMEM,
        scratch_shapes=move_scratch(rows, block, before.shape[1]),
        compiler_params=pltpu.CompilerParams(collective_id=1, has_side_effects=True, vmem_limit_bytes=GRANT),
        name="last_round",
    )(blocks, before, after, rotation)


def pick_kernel(embedding, pairing, picked):
    block = picked.shape[3]

    def one(target, _):
        for half in range(2):
            source = pl.multiple_of(pairing[2 * target + half] * block, block)
            picked[target, half] = embedding[:, pl.ds(source, block)]
        return 0

    lax.fori_loop(0, picked.shape[0], one, 0, unroll=4)


def pick(embedding, pairing):
    sub_rows, columns = embedding.shape
    slots = pairing.shape[0]
    return pl.pallas_call(
        pick_kernel,
        out_shape=jax.ShapeDtypeStruct((slots // 2, 2, sub_rows, columns // slots), F32),
        in_specs=[VMEM, pl.BlockSpec(memory_space=pltpu.SMEM)],
        out_specs=VMEM,
        compiler_params=pltpu.CompilerParams(vmem_limit_bytes=GRANT),
        name="pick",
    )(embedding, pairing)


def deal_kernel(
    grid, cut, outgoing, blocks, gram, before, after, high_sum, side_sum, send, recv, own, raw_send, raw_recv,
    part, total, slots, sums, sum_send, sum_recv,
):
    tall, ring, cores = cut
    sub_rows = outgoing.shape[2]
    block = blocks.shape[2]
    devices = lax.axis_size("pair")
    me = lax.axis_index("pair")
    core, turn, side = me % cores, me // cores % ring, me // (cores * ring)
    halfway = ring // 2
    group = tall * cores

    def device(there_side, there_turn, there_core):
        return (there_side % tall * ring + (there_turn + 2 * ring) % ring) * cores + there_core % cores

    def target_of(far, near):
        return device(side + near // cores, turn + far, core + near % cores)

    def rows_of(index):
        return pl.ds(pl.multiple_of(index * sub_rows, sub_rows), sub_rows)

    def far_of(order):
        away = (order + 1) // 2
        return halfway + away - 2 * away * (order % 2)

    def copy_at(far, near):
        target = target_of(far, near)
        step = far * group + near
        return pltpu.make_async_remote_copy(
            outgoing.at[target], blocks.at[:, rows_of(me), :], send.at[step], recv.at[step], {"pair": target}, MESH
        )

    barrier = pltpu.get_barrier_semaphore()

    def call(step, _):
        target = target_of(step // group, step % group)
        pl.semaphore_signal(barrier, inc=1, device_id={"pair": target}, device_id_type=MESH)
        return 0

    lax.fori_loop(1, devices, call, 0)
    across = row_peers(grid)
    greet(across)
    keep = pltpu.make_async_copy(outgoing.at[me], blocks.at[:, rows_of(me), :], own)
    keep.start()
    met(devices - 1 + len(across))
    def send_all(order, _):
        for near in range(group):
            copy_at(far_of(order), near).start()
        return 0

    lax.fori_loop(0, ring - 1, send_all, 0)
    for near in range(1, group):
        copy_at(0, near).start()
    keep.wait()
    high_sum[...] = jnp.zeros_like(high_sum)
    side_sum[...] = jnp.zeros_like(side_sum)

    def add(order, _):
        far = far_of(order)
        for near in range(group):

            @pl.when(far * group + near > 0)
            def _(near=near):
                copy_at(far, near).wait_recv()

        pieces = []
        for there in range(tall):
            source = (there * ring + (turn - far + ring) % ring) * cores
            rows = pl.ds(pl.multiple_of(source * sub_rows, sub_rows * cores), sub_rows * cores)
            pieces.append(jnp.concatenate([blocks[0, rows, :], blocks[1, rows, :]], axis=1))
        high, low = halves(jnp.concatenate(pieces, axis=0))

        def one(x, y):
            return lax.dot_general(x, y, (((0,), (0,)), ((), ())), preferred_element_type=F32)

        high_sum[...] += one(high, high)
        side_sum[...] += one(high, low)
        return 0

    lax.fori_loop(0, ring, add, 0)
    mixed = side_sum[...]
    whole = high_sum[...] + (mixed + mixed.T)
    part[:block, :] = whole[:block, :block]
    part[block : 2 * block, :] = whole[:block, block:]
    part[2 * block :, :] = whole[block:, block:]
    position, first, last, _, _ = pair_place()

    begin, beside, raws_finish = raw_moves(
        blocks, before, after, raw_send, raw_recv, position, first, last, ring * cores
    )
    begin()
    row_total(grid, GRAM_STREAMS, part, total, slots, sums, sum_send, sum_recv, beside)
    gram[:block, :block] = total[:block, :]
    gram[:block, block:] = total[block : 2 * block, :]
    gram[block:, :block] = total[block : 2 * block, :].T
    gram[block:, block:] = total[2 * block :, :]

    raws_finish()

    def sent(step, _):
        copy_at(step // group, step % group).wait_send()
        return 0

    lax.fori_loop(1, devices, sent, 0)


def deal(picked, grid, cut):
    devices, _, sub_rows, block = picked.shape
    return pl.pallas_call(
        functools.partial(deal_kernel, grid, cut),
        out_shape=(
            jax.ShapeDtypeStruct((2, sub_rows * devices, block), F32),
            jax.ShapeDtypeStruct((2 * block, 2 * block), F32),
            raw_shape(DEAL_AHEAD, block),
            raw_shape(DEAL_AHEAD, block),
        ),
        in_specs=[VMEM],
        out_specs=(VMEM,) * 4,
        scratch_shapes=[
            pltpu.VMEM((2 * block, 2 * block), F32),
            pltpu.VMEM((2 * block, 2 * block), F32),
            pltpu.SemaphoreType.DMA((devices,)),
            pltpu.SemaphoreType.DMA((devices,)),
            pltpu.SemaphoreType.DMA,
            pltpu.SemaphoreType.DMA((2, 2 * DEAL_AHEAD)),
            pltpu.SemaphoreType.DMA((2, 2 * DEAL_AHEAD)),
        ]
        + total_scratch(grid, GRAM_STREAMS, 3 * block, block),
        compiler_params=pltpu.CompilerParams(collective_id=0, has_side_effects=True, vmem_limit_bytes=GRANT),
        name="deal",
    )(picked)


def join_kernel(blocks, joined, sems):
    block = blocks.shape[2]
    parts = sems.shape[1]
    rows = blocks.shape[1] // parts
    copies = []
    for half in range(2):
        for part in range(parts):
            here = pl.ds(part * rows, rows)
            copies.append(
                pltpu.make_async_copy(
                    blocks.at[half, here], joined.at[here, pl.ds(half * block, block)], sems.at[half, part]
                )
            )
            copies[-1].start()
    for copy in copies:
        copy.wait()


def join(blocks):
    _, rows, block = blocks.shape
    return pl.pallas_call(
        join_kernel,
        out_shape=jax.ShapeDtypeStruct((rows, 2 * block), F32),
        in_specs=[pl.BlockSpec(memory_space=pl.ANY)],
        out_specs=pl.BlockSpec(memory_space=pltpu.HBM),
        scratch_shapes=[pltpu.SemaphoreType.DMA((2, 4))],
        compiler_params=pltpu.CompilerParams(vmem_limit_bytes=GRANT),
        name="join",
    )(blocks)


def cuts():
    grids = {16: (4, 4), 4: (2, 2)}
    pairs = {32: (2, 8, 2), 4: (1, 2, 2)}
    return grids[lax.axis_size("row")], pairs[lax.axis_size("pair")]


def body(embedding, pairing):
    grid, cut = cuts()
    blocks, gram, before, after = deal(pick(embedding, pairing), grid, cut)
    total_rows = blocks.shape[1] * lax.axis_size("row")
    for round_num in range(ROUNDS):
        rotation, upper_gram, lower_gram = make_rotation(gram, total_rows)
        if round_num + 1 < ROUNDS:
            blocks, gram, before, after = next_round(
                blocks, before, after, rotation, upper_gram, lower_gram, grid, cut[1] * cut[2], 2 + round_num
            )
        else:
            blocks = last_round(blocks, before, after, rotation)
    return join(blocks)


def solution(mesh):
    in_specs = (P(("row", "pair"), None), P())
    out_specs = P("row", "pair")
    return jax.shard_map(body, mesh=mesh, in_specs=in_specs, out_specs=out_specs, check_vma=False)
```
